32 devices in a mesh: seq: 8 (over z, y), tp: 4 (over x, core).
Axes of the slice: x: 2, y: 2, z: 4, core: 2. Of those that a mesh axis runs over, the one named last changes fastest.
Arguments:
- inner_x: bfloat16 [2048, 8192], P('seq', 'tp'), may hold values from -6 to 6
- in_b: bfloat16 [2048, 1024], P('seq', 'tp'), may hold values from -6 to 6
- in_c: bfloat16 [2048, 1024], P('seq', 'tp'), may hold values from -6 to 6
- log_decay: float32 [128, 2048], P('tp', 'seq'), may hold values from -2 to 0
- doc_lengths: int32 [4], replicated, may hold values from 1 to 1024, 2048 in all
- out_grad: bfloat16 [2048, 8192], P('seq', 'tp'), may hold values from -0.0016937256 to 0.0016937256
- w_b: bfloat16 [8192, 1024], P(None, 'tp'), may hold values from -0.09375 to 0.09375
- w_c: bfloat16 [8192, 1024], P(None, 'tp'), may hold values from -0.0625 to 0.0625
Outputs:
- grad_x: bfloat16 [2048, 8192], P('seq', 'tp')
- grad_input: bfloat16 [2048, 8192], P('seq', 'tp')
The draws below stay inside these ranges and needn't reach their ends.
Inputs may be any that keep to these rules, and one draw needn't show every extreme that they name: `doc_lengths`: the lengths sum to 2048; the longest is exactly half of 2048.
All inputs are finite; a program needn't handle non-finite values.
Results may differ from the reference program's by a relative error of at most 0.023.
Values may be sent and summed in bfloat16 or wider, within the bound.
A program may use at most 128 MiB of HBM per device.

```python
import math
import jax
import jax.numpy as jnp
import numpy as np
from jax import lax

D = 8192
SPACE_HEADS = 128
HEAD_DIM = 64
STATE = 128
GROUPS = 8
SPAN = 128
TOK_DEV = 256
DOCS = 4
SEQUENCE_TOKENS = 2048
INNER = 8192
BC_WIDTH = 1024
N_TP = 4


def draw_log_decay(key, part):
    random_key_series = jax.random.split(jax.random.fold_in(key, 7), 8)
    mixed_share = 0.5
    mixed_heads = jax.random.bernoulli(random_key_series[0], mixed_share, (SPACE_HEADS,))
    device_fast = jax.random.bernoulli(random_key_series[7], 0.5, (SPACE_HEADS, SEQUENCE_TOKENS // TOK_DEV))
    device_fast = jnp.repeat(device_fast, TOK_DEV, axis=1)
    fast_tokens = jnp.logical_and(mixed_heads[:, None], device_fast)
    fast_rate = jnp.exp(jax.random.uniform(random_key_series[1], (SPACE_HEADS,), jnp.float32, math.log(1.0 / 50.0), math.log(1.0 / 30.0)))
    slow_rate = jnp.exp(jax.random.uniform(random_key_series[2], (SPACE_HEADS,), jnp.float32, math.log(0.02), math.log(0.12))) / SEQUENCE_TOKENS
    token_rate = jnp.where(fast_tokens, fast_rate[:, None], slow_rate[:, None])
    block_multiplier = jnp.exp(jax.random.uniform(random_key_series[3], (SPACE_HEADS, SEQUENCE_TOKENS // SPAN), jnp.float32, math.log(0.5), math.log(2.0)))
    block_multiplier = jnp.repeat(block_multiplier, SPAN, axis=1)
    position_multiplier = jax.random.uniform(random_key_series[4], (SPACE_HEADS, SEQUENCE_TOKENS), jnp.float32, 0.5, 2.0)
    surge_position = jax.random.randint(random_key_series[5], (3,), 0, SEQUENCE_TOKENS)
    surge_length = jax.random.uniform(random_key_series[6], (SPACE_HEADS, 1), jnp.float32, 0.22, 0.69)
    surge_matches = jnp.sum((jnp.arange(SEQUENCE_TOKENS)[None, :] == surge_position[:, None]).astype(jnp.float32), axis=0)
    return -(token_rate * block_multiplier * position_multiplier) - surge_length * surge_matches[None, :]


def strengthened(result, rng, source, target, parts, factor):
    owner, partner = [(jnp.arange(result.shape[axis_at]) // (result.shape[axis_at] // parts)).reshape([-1 if axis == axis_at else 1 for axis in range(result.ndim)]) for axis_at in (source, target)]
    chosen = jax.random.permutation(rng, parts)[partner]
    strong = (owner == chosen) | (owner == (partner + parts // 2) % parts)
    return jnp.where(strong, factor * result, result)


def levels(stream_key, dims, cuts, low, top_value):
    loudness, own = 1.0, jax.random.fold_in(stream_key, 6)
    for dim, parts in cuts:
        draws = jnp.exp(jax.random.uniform(jax.random.fold_in(own, dim), (parts,), jnp.float32, low / len(cuts), top_value / len(cuts)))
        loudness = loudness * jnp.repeat(draws, dims[dim] // parts).reshape([-1 if axis == dim else 1 for axis in range(len(dims))])
    return loudness


def profile(number_of, total, limit, skew):
    loads = [(1 << 20) // math.isqrt(rank ** skew) + 1 for rank in range(2, number_of + 1)]
    surplus, given = total - limit - (number_of - 1), [1] * (number_of - 1)
    while surplus > 0:
        movable = [i for i in range(number_of - 1) if given[i] < limit]
        pool, budget = sum([loads[i] for i in movable]), surplus
        for i in movable:
            extra = min(limit - given[i], max(1, budget * loads[i] // pool), surplus)
            given[i] = given[i] + extra
            surplus = surplus - extra
    return np.array([limit] + given)


def ragged_sizes(key, number_of, total, bound, skew):
    if number_of == 2:
        one = jax.random.randint(key, (), max(1, total - bound), min(bound, total - 1) + 1)
        return jnp.stack([one, total - one])
    sizes = jnp.asarray(profile(number_of, total, bound, skew), jnp.int32)
    pairs = (number_of - 1) // 2
    giver, taker = sizes[1:1 + 2 * pairs:2], sizes[2:2 + 2 * pairs:2]
    margin = jnp.minimum(giver - 1, bound - taker)
    passed = jax.random.randint(jax.random.fold_in(key, 1), (pairs,), 0, 1 << 20) % (margin + 1)
    sizes = sizes.at[1:1 + 2 * pairs:2].set(giver - passed).at[2:2 + 2 * pairs:2].set(taker + passed)
    return sizes[jax.random.permutation(jax.random.fold_in(key, 2), number_of)]


def normal_values(rng, shape, width, limit, pieces=(), kind=jnp.bfloat16):
    result = width * jax.random.normal(rng, shape, jnp.float32)
    if pieces:
        result = result * levels(rng, shape, pieces, -0.22, 0.18)
    return jnp.clip(result, -limit, limit).astype(kind)


def bell_draw_with(rng, dims, width, bound, shards, heavy, held_as=jnp.bfloat16):
    array = width * jax.random.normal(rng, dims, jnp.float32)
    if shards:
        array = array * levels(rng, dims, shards, -0.22, 0.18)
    return jnp.clip(strengthened(array, jax.random.fold_in(rng, 3), *heavy), -bound, bound).astype(held_as)


def setup_inputs(seed: int = 0) -> dict:
    key_of = jax.random.split(jax.random.key(seed), 9)
    return {
        "inner_x": normal_values(key_of[0], (SEQUENCE_TOKENS, INNER), 1.0, 6.0, ((0, 8), (1, 4))),
        "in_b": normal_values(key_of[1], (SEQUENCE_TOKENS, BC_WIDTH), 1.0, 6.0, ((0, 8), (1, 4))),
        "in_c": normal_values(key_of[2], (SEQUENCE_TOKENS, BC_WIDTH), 1.0, 6.0, ((0, 8), (1, 4))),
        "log_decay": draw_log_decay(jax.random.fold_in(key_of[8], 71), 0),
        "doc_lengths": ragged_sizes(key_of[4], DOCS, SEQUENCE_TOKENS, SEQUENCE_TOKENS // 2, 2).astype(jnp.int32),
        "out_grad": jnp.clip(jax.random.uniform(key_of[5], (SEQUENCE_TOKENS, INNER), jnp.float32, -0.0016937256, 0.0016937256) * levels(key_of[5], (SEQUENCE_TOKENS, INNER), ((0, 8), (1, 4)), -0.4, 0.0), -0.0016937256, 0.0016937256).astype(jnp.bfloat16),
        "w_b": bell_draw_with(key_of[6], (D, BC_WIDTH), D ** -0.5, 0.09375, ((1, 4),), (1, 0, 4, 2.0)),
        "w_c": normal_values(key_of[7], (D, BC_WIDTH), D ** -0.5, 0.0625, ((1, 4),)),
    }


def doc_ids(doc_lengths, positions):
    doc_ends = jnp.cumsum(doc_lengths)[:-1]
    return jnp.sum((positions[:, None] >= doc_ends[None, :]).astype(jnp.int32), axis=1).astype(jnp.int32)


def span_vectors(log_part, doc_part, doc_prior):
    cumulative = jnp.cumsum(log_part, axis=-1)
    decay_enter = jnp.where(doc_part == doc_prior, jnp.exp(cumulative), 0.0)
    decay_leave = jnp.where(doc_part == doc_part[-1], jnp.exp(cumulative[..., -1:] - cumulative), 0.0)
    decay_total = jnp.where(doc_part[-1] == doc_prior, jnp.exp(cumulative[..., -1]), 0.0)
    return decay_enter, decay_leave, decay_total


def span_within(log_part, doc_part):
    cumulative = jnp.cumsum(log_part, axis=-1)
    span_len = doc_part.shape[0]
    row_ids = jnp.arange(span_len)
    same_doc = (doc_part[:, None] == doc_part[None, :]) & (row_ids[:, None] >= row_ids[None, :])
    log_gaps = cumulative[..., :, None] - cumulative[..., None, :]
    return jnp.where(same_doc, jnp.exp(jnp.where(same_doc, log_gaps, 0.0)), 0.0)


def weigh_rows(x_part, dy_part, decay_enter, decay_leave):
    leave_rows = jnp.transpose(decay_leave, (2, 0, 1))[..., None]
    enter_rows = jnp.transpose(decay_enter, (2, 0, 1))[..., None]
    x_weighted = (x_part.astype(jnp.float32) * leave_rows).astype(jnp.bfloat16)
    dy_weighted = (dy_part.astype(jnp.float32) * enter_rows).astype(jnp.bfloat16)
    return x_weighted, dy_weighted


def span_summary(x_weighted, dy_weighted, b_part, c_part):
    local_state = jnp.einsum("lghp,lgn->ghpn", x_weighted, b_part, preferred_element_type=jnp.float32)
    local_grad = jnp.einsum("lghp,lgn->ghpn", dy_weighted, c_part, preferred_element_type=jnp.float32)
    return local_state, local_grad


def span_grads(x_part, dy_part, b_part, c_part, x_weighted, dy_weighted, within, decay_leave, start_state, end_grad):
    pair_scores = jnp.einsum("ign,jgn->gij", c_part, b_part, preferred_element_type=jnp.float32)
    inner_dots = jnp.einsum("ighp,jghp->ghij", dy_part, x_part, preferred_element_type=jnp.float32)
    score_low = (within * pair_scores[:, None]).astype(jnp.bfloat16)
    leave_rows = jnp.transpose(decay_leave, (2, 0, 1))[..., None]
    end_low = end_grad.astype(jnp.bfloat16)
    start_low = start_state.astype(jnp.bfloat16)
    grad_x = jnp.einsum("ghij,ighp->jghp", score_low, dy_part, preferred_element_type=jnp.float32)
    grad_x = grad_x + jnp.einsum("jgn,ghpn->jghp", b_part, end_low, preferred_element_type=jnp.float32) * leave_rows
    mixed_low = jnp.sum(within * inner_dots, axis=1).astype(jnp.bfloat16)
    grad_c = jnp.einsum("gij,jgn->ign", mixed_low, b_part, preferred_element_type=jnp.float32)
    grad_c = grad_c + jnp.einsum("ighp,ghpn->ign", dy_weighted, start_low, preferred_element_type=jnp.float32)
    grad_b = jnp.einsum("gij,ign->jgn", mixed_low, c_part, preferred_element_type=jnp.float32)
    grad_b = grad_b + jnp.einsum("jghp,ghpn->jgn", x_weighted, end_low, preferred_element_type=jnp.float32)
    return grad_x, grad_b, grad_c


def reference(inner_x, in_b, in_c, log_decay, doc_lengths, out_grad, w_b, w_c):
    per_group = SPACE_HEADS // GROUPS
    span_count = SEQUENCE_TOKENS // SPAN
    x_parts = inner_x.reshape(span_count, SPAN, GROUPS, per_group, HEAD_DIM)
    dy_parts = out_grad.reshape(span_count, SPAN, GROUPS, per_group, HEAD_DIM)
    b_parts = in_b.reshape(span_count, SPAN, GROUPS, STATE)
    c_parts = in_c.reshape(span_count, SPAN, GROUPS, STATE)
    log_parts = jnp.transpose(log_decay.reshape(GROUPS, per_group, span_count, SPAN), (2, 0, 1, 3))
    doc_all = doc_ids(doc_lengths, jnp.arange(SEQUENCE_TOKENS, dtype=jnp.int32))
    doc_parts = doc_all.reshape(span_count, SPAN)
    doc_priors = jnp.concatenate([jnp.full((1,), -1, jnp.int32), doc_parts[:-1, -1].astype(jnp.int32)])
    zero_state = jnp.zeros((GROUPS, per_group, HEAD_DIM, STATE), jnp.float32)

    def forward(carried, span_item):
        x_part, dy_part, b_part, c_part, log_part, doc_part, doc_prior = span_item
        decay_enter, decay_leave, decay_total = span_vectors(log_part, doc_part, doc_prior)
        x_weighted, dy_weighted = weigh_rows(x_part, dy_part, decay_enter, decay_leave)
        local_state, local_grad = span_summary(x_weighted, dy_weighted, b_part, c_part)
        updated = decay_total[..., None, None] * carried + local_state
        return updated, carried

    items = (x_parts, dy_parts, b_parts, c_parts, log_parts, doc_parts, doc_priors)
    unused, start_states = lax.scan(forward, zero_state, items)

    def backward(carried, span_item):
        x_part, dy_part, b_part, c_part, log_part, doc_part, doc_prior, start_state = span_item
        decay_enter, decay_leave, decay_total = span_vectors(log_part, doc_part, doc_prior)
        x_weighted, dy_weighted = weigh_rows(x_part, dy_part, decay_enter, decay_leave)
        within = span_within(log_part, doc_part)
        grads = span_grads(x_part, dy_part, b_part, c_part, x_weighted, dy_weighted, within, decay_leave, start_state, carried)
        local_state, local_grad = span_summary(x_weighted, dy_weighted, b_part, c_part)
        updated = decay_total[..., None, None] * carried + local_grad
        return updated, grads

    unused_grad, outputs = lax.scan(backward, zero_state, items + (start_states,), reverse=True)
    grad_x = outputs[0].reshape(SEQUENCE_TOKENS, SPACE_HEADS * HEAD_DIM).astype(jnp.bfloat16)
    grad_b = outputs[1].reshape(SEQUENCE_TOKENS, GROUPS * STATE).astype(jnp.bfloat16)
    grad_c = outputs[2].reshape(SEQUENCE_TOKENS, GROUPS * STATE).astype(jnp.bfloat16)
    block_width = GROUPS * STATE // N_TP
    summed = jnp.zeros((SEQUENCE_TOKENS, D), jnp.float32)
    for number in range(N_TP):
        low = number * block_width
        high = low + block_width
        partial_value = lax.dot_general(grad_b[:, low:high], w_b[:, low:high], (((1,), (1,)), ((), ())), preferred_element_type=jnp.float32)
        partial_value = partial_value + lax.dot_general(grad_c[:, low:high], w_c[:, low:high], (((1,), (1,)), ((), ())), preferred_element_type=jnp.float32)
        summed = summed + lax.optimization_barrier(partial_value.astype(jnp.bfloat16)).astype(jnp.float32)
    return grad_x, summed.astype(jnp.bfloat16)
```

```python
import functools

import jax
import jax.numpy as jnp
from jax import lax
from jax.experimental import pallas as pl
from jax.experimental.pallas import tpu as pltpu
from jax.sharding import PartitionSpec as P

HEAD_DIM = 64
STATE = 128
SPAN = 128
LAG = 5
WAIT = 6
F32 = jnp.float32
BF16 = jnp.bfloat16
MESH = pl.DeviceIdType.MESH
SMEM = pl.BlockSpec(memory_space=pltpu.SMEM)
ANY = pl.BlockSpec(memory_space=pl.ANY)


def dot(a, b, a_dim, b_dim):
    return lax.dot_general(a, b, (((a_dim,), (b_dim,)), ((), ())), preferred_element_type=F32)


def doc_of(lens_ref, position):
    end = 0
    doc = jnp.zeros_like(position)
    for k in range(lens_ref.shape[0] - 1):
        end = end + lens_ref[k]
        doc = doc + (position >= end).astype(jnp.int32)
    return doc


def span_decays(lens_ref, log_ref, number):
    heads, tokens = log_ref.shape
    first = lax.axis_index("seq") * tokens + number * SPAN
    cumulative = log_ref[:, number * SPAN : (number + 1) * SPAN]
    lane = lax.broadcasted_iota(jnp.int32, (heads, SPAN), 1)
    shift = 1
    while shift < SPAN:
        rolled = pltpu.roll(cumulative, shift, 1)
        cumulative = cumulative + jnp.where(lane >= shift, rolled, 0.0)
        shift *= 2
    doc_row = doc_of(lens_ref, first + lane)
    doc_last = doc_of(lens_ref, jnp.full((heads, SPAN), first + SPAN - 1, jnp.int32))
    before = jnp.full((heads, SPAN), first - 1, jnp.int32)
    doc_prior = jnp.where(before >= 0, doc_of(lens_ref, before), -1)
    last = jnp.broadcast_to(cumulative[:, SPAN - 1 :], (heads, SPAN))
    enter = jnp.where(doc_row == doc_prior, jnp.exp(cumulative), 0.0)
    leave = jnp.where(doc_row == doc_last, jnp.exp(last - cumulative), 0.0)
    total = jnp.where(doc_last == doc_prior, jnp.exp(last), 0.0)
    return cumulative, enter, leave, total


def fused_kernel(
    columns, chips, pieces, lens_ref, x_hbm, dy_hbm, b_hbm, c_hbm, log_hbm, wb_ref, wc_ref, gx_ref, out_ref,
    x_ref, dy_ref, b_ref, c_ref, log_ref, turned, totals, d_ref, d_prev, d_next, bias, scores, mixed,
    xw_ref, dyw_ref, gx_local, gb_ref, gc_ref, gbc_ref, f0_ref, f_ref, g1_ref, g_ref,
    c_in, c_out, c_side, b_in, b_out, b_side,
    w_all, pair_out, pair_in, chip_out, chip_in,
    load_sems, d_sems, send_sems, recv_sems,
    w_sems, pair_send, pair_recv, chip_send, chip_recv,
):
    heads = log_ref.shape[0]
    groups = b_ref.shape[1] // STATE
    chunks = heads // 2
    pairs = chunks // groups
    width = 2 * HEAD_DIM
    k = lax.axis_index("seq")
    m = k // 2
    r = k - 2 * m
    devices = 2 * columns
    partner = k + 1 - 2 * r
    t = lax.axis_index("tp")
    chip = t // 2
    core = t - 2 * chip
    mate = t + 1 - 2 * core
    block = out_ref.shape[1]
    piece = block // pieces
    depth = wb_ref.shape[1]

    barrier = pltpu.get_barrier_semaphore()
    for offset in (-2, -1, 1, 2):
        @pl.when(jnp.logical_and(k + offset >= 0, k + offset < devices))
        def _():
            pl.semaphore_signal(
                barrier, inc=1, device_id={"seq": k + offset, "tp": t}, device_id_type=MESH
            )

    def owner_of(offset, same_core):
        at = lax.rem(chip + offset, chips)
        return 2 * at + (core if same_core else 1 - core)

    pl.semaphore_signal(barrier, inc=1, device_id={"seq": k, "tp": mate}, device_id_type=MESH)
    for offset in range(1, chips):
        pl.semaphore_signal(
            barrier, inc=1, device_id={"seq": k, "tp": owner_of(offset, True)}, device_id_type=MESH
        )

    quarter = x_ref.shape[1] // 4
    loads = [
        pltpu.make_async_copy(log_hbm, log_ref, load_sems.at[0]),
        pltpu.make_async_copy(b_hbm, b_ref, load_sems.at[1]),
        pltpu.make_async_copy(c_hbm, c_ref, load_sems.at[2]),
    ]
    for q in range(4):
        cols = pl.ds(q * quarter, quarter)
        loads.append(pltpu.make_async_copy(x_hbm.at[:, cols], x_ref.at[:, cols], load_sems.at[3 + 2 * q]))
        loads.append(pltpu.make_async_copy(dy_hbm.at[:, cols], dy_ref.at[:, cols], load_sems.at[4 + 2 * q]))
    for load in loads:
        load.start()

    def w_copy(offset, same_core, c, which):
        at = pl.multiple_of(owner_of(offset, same_core) * block + c * piece, piece)
        slot = (offset * 2 + (1 if same_core else 0)) * pieces + c
        return pltpu.make_async_copy(
            (wb_ref, wc_ref)[which].at[pl.ds(at, piece)],
            w_all.at[slot, :, pl.ds(which * depth, depth)],
            w_sems.at[slot, which],
        )

    for offset in range(chips):
        def fetch(c, carry):
            for same_core in (False, True):
                for which in (0, 1):
                    w_copy(offset, same_core, c, which).start()
            return carry

        lax.fori_loop(0, pieces, fetch, 0)

    loads[0].wait()
    low = lax.broadcasted_iota(jnp.int32, (SPAN, width), 1) < HEAD_DIM
    low_mask = low.astype(F32).astype(BF16)
    high_mask = (1.0 - low.astype(F32)).astype(BF16)
    row_id = lax.broadcasted_iota(jnp.int32, (SPAN, SPAN), 0)
    col_id = lax.broadcasted_iota(jnp.int32, (SPAN, SPAN), 1)
    for number in range(2):
        cumulative, enter, leave, total = span_decays(lens_ref, log_ref, number)
        log_ref[:, number * SPAN : (number + 1) * SPAN] = cumulative
        turned[3 * number] = jnp.transpose(cumulative)
        turned[3 * number + 1] = jnp.transpose(enter)
        turned[3 * number + 2] = jnp.transpose(leave)
        totals[number] = total
        first = k * log_ref.shape[1] + number * SPAN
        same = jnp.logical_and(
            doc_of(lens_ref, first + row_id) == doc_of(lens_ref, first + col_id), row_id >= col_id
        )
        bias[number] = jnp.where(same, 0.0, -1e30)
    both = totals[0] * totals[1]
    for h in range(heads):
        d_ref[h] = both[h : h + 1, :]

    count = jnp.minimum(k, 2) + jnp.minimum(devices - 1 - k, 2) + chips
    pl.semaphore_wait(barrier, count)

    def copy(stream, c, source, target, to):
        rows = pl.ds(pl.multiple_of(c * width, width), width)
        return pltpu.make_async_remote_copy(
            src_ref=source.at[rows], dst_ref=target.at[rows],
            send_sem=send_sems.at[stream, c], recv_sem=recv_sems.at[stream, c],
            device_id={"seq": to, "tp": t}, device_id_type=MESH,
        )

    def decay_copy(stream, target, to):
        return pltpu.make_async_remote_copy(
            src_ref=d_ref, dst_ref=target,
            send_sem=d_sems.at[0, stream], recv_sem=d_sems.at[1, stream],
            device_id={"seq": to, "tp": t}, device_id_type=MESH,
        )

    to_next = decay_copy(0, d_prev, k + 1)
    to_prev = decay_copy(1, d_next, k - 1)
    sends_next = jnp.logical_and(k + 1 >= 2, k + 1 < devices)
    sends_prev = jnp.logical_and(k >= 1, k - 1 <= devices - 3)

    @pl.when(sends_next)
    def _():
        to_next.start()

    @pl.when(sends_prev)
    def _():
        to_prev.start()

    loads[1].wait()
    loads[2].wait()

    def spans(number):
        return slice(number * SPAN, (number + 1) * SPAN)

    def spread(kind, number, pair):
        held = turned.at[3 * number + kind]
        one = jnp.broadcast_to(held[:, 2 * pair : 2 * pair + 1], (SPAN, width))
        two = jnp.broadcast_to(held[:, 2 * pair + 1 : 2 * pair + 2], (SPAN, width))
        return jnp.where(low, one, two)

    def by_head(number, pair):
        return jnp.concatenate(
            [
                jnp.broadcast_to(totals[number, h : h + 1, :], (HEAD_DIM, STATE))
                for h in (2 * pair, 2 * pair + 1)
            ],
            axis=0,
        )

    def summarize(pair):
        group = pair // pairs
        cols = slice(pair * width, (pair + 1) * width)
        cols_g = slice(group * STATE, (group + 1) * STATE)
        states, grads = [], []
        for number in (0, 1):
            tokens = spans(number)
            x_weighted = (x_ref[tokens, cols].astype(F32) * spread(2, number, pair)).astype(BF16)
            dy_weighted = (dy_ref[tokens, cols].astype(F32) * spread(1, number, pair)).astype(BF16)
            xw_ref[tokens, cols] = x_weighted
            dyw_ref[tokens, cols] = dy_weighted
            states.append(dot(x_weighted, b_ref[tokens, cols_g], 0, 0))
            grads.append(dot(dy_weighted, c_ref[tokens, cols_g], 0, 0))
        f0_ref[cols] = states[0]
        f_ref[cols] = states[1] + by_head(1, pair) * states[0]
        g1_ref[cols] = grads[1]
        g_ref[cols] = grads[0] + by_head(0, pair) * grads[1]

    def local(pair):
        group = pair // pairs
        cols = slice(pair * width, (pair + 1) * width)
        cols_g = slice(group * STATE, (group + 1) * STATE)
        for number in (0, 1):
            tokens = spans(number)
            slot = 2 * group + number
            if pair == group * pairs:
                scores[slot] = dot(c_ref[tokens, cols_g], b_ref[tokens, cols_g], 1, 1)
            x_part, dy_part = x_ref[tokens, cols], dy_ref[tokens, cols]
            x_blocks = jnp.concatenate([x_part * low_mask, x_part * high_mask], axis=0)
            dy_blocks = jnp.concatenate([dy_part * low_mask, dy_part * high_mask], axis=0)
            dots = dot(dy_part, x_blocks, 1, 1)
            score_low = []
            added = None
            for e in range(2):
                h = 2 * pair + e
                column = jnp.broadcast_to(turned[3 * number, :, h : h + 1], (SPAN, SPAN))
                gap = column - log_ref[h : h + 1, number * SPAN : (number + 1) * SPAN]
                within = jnp.exp(gap + bias[number])
                term = within * dots[:, e * SPAN : (e + 1) * SPAN]
                added = term if added is None else added + term
                score_low.append((within * scores[slot]).astype(BF16))
            mixed[slot] = added if pair == group * pairs else mixed[slot] + added
            gx_local[tokens, cols] = dot(jnp.concatenate(score_low, axis=0), dy_blocks, 0, 0)
            if pair == group * pairs + pairs - 1:
                mixed_low = mixed[slot].astype(BF16)
                gb_ref[tokens, cols_g] = dot(mixed_low, c_ref[tokens, cols_g], 0, 0)
                gc_ref[tokens, cols_g] = dot(mixed_low, b_ref[tokens, cols_g], 1, 0)

    def stream(base, has_in, has_next, ahead, source, buf_in, buf_out, buf_side, near, arrival, passes_own):
        chain = lambda c: copy(base, c, buf_out, buf_in, ahead)
        side_own = lambda c: copy(base + 1, c, buf_out, buf_side, partner)
        side_in = lambda c: copy(base + 1, c, buf_in, buf_side, partner)
        passes_in = jnp.logical_and(jnp.logical_not(passes_own), has_in)
        side_arrives = jnp.logical_or(jnp.logical_not(passes_own), has_in)

        def step(c):
            @pl.when(jnp.logical_and(has_in, c == 0))
            def _():
                arrival.wait_recv()

            @pl.when(has_in)
            def _():
                chain(c).wait_recv()

                @pl.when(jnp.logical_not(passes_own))
                def _():
                    side_in(c).start()

                for e in range(2):
                    h = 2 * c + e
                    rows = pl.ds(pl.multiple_of(h * HEAD_DIM, HEAD_DIM), HEAD_DIM)
                    product = d_ref[h] * near[h]
                    buf_out[rows, :] = (source[rows, :] + product * buf_in[rows, :].astype(F32)).astype(BF16)

            @pl.when(jnp.logical_not(has_in))
            def _():
                rows = pl.ds(pl.multiple_of(c * width, width), width)
                buf_out[rows, :] = source[rows, :].astype(BF16)

            @pl.when(passes_own)
            def _():
                side_own(c).start()

            @pl.when(has_next)
            def _():
                chain(c).start()

        def finish(c):
            @pl.when(side_arrives)
            def _():
                side_own(c).wait_recv()

            for e in range(2):
                h = 2 * c + e
                rows = slice(h * HEAD_DIM, (h + 1) * HEAD_DIM)

                @pl.when(has_in)
                def _():
                    source[rows, :] = (
                        buf_side[rows, :].astype(F32) + near[h] * buf_in[rows, :].astype(F32)
                    )

                @pl.when(jnp.logical_and(jnp.logical_not(has_in), side_arrives))
                def _():
                    source[rows, :] = buf_side[rows, :].astype(F32)

                @pl.when(jnp.logical_not(side_arrives))
                def _():
                    source[rows, :] = jnp.zeros((HEAD_DIM, STATE), F32)

        def drain(c):
            @pl.when(has_next)
            def _():
                chain(c).wait_send()

            @pl.when(jnp.logical_or(passes_own, passes_in))
            def _():
                side_own(c).wait_send()

        return step, finish, drain

    forward, forward_end, forward_drain = stream(
        0, m > 0, m < columns - 1, k + 2, f_ref, c_in, c_out, c_side, d_prev, to_next, r == 0
    )
    backward, backward_end, backward_drain = stream(
        2, m < columns - 1, m > 0, k - 2, g_ref, b_in, b_out, b_side, d_next, to_prev, r == 1
    )
    lead = LAG * (columns - 1 - 2 * m)
    forward_at = jnp.maximum(-lead, 0)
    backward_at = jnp.maximum(lead, 0)

    def carried(pair):
        group = pair // pairs
        cols = slice(pair * width, (pair + 1) * width)
        cols_g = slice(group * STATE, (group + 1) * STATE)
        forward_end(pair)
        backward_end(pair)
        arrived, ended = f_ref[cols], g_ref[cols]
        starts = [arrived.astype(BF16), (f0_ref[cols] + by_head(0, pair) * arrived).astype(BF16)]
        ends = [(g1_ref[cols] + by_head(1, pair) * ended).astype(BF16), ended.astype(BF16)]
        for number in (0, 1):
            tokens = spans(number)
            grad_x = gx_local[tokens, cols] + spread(2, number, pair) * dot(
                b_ref[tokens, cols_g], ends[number], 1, 1
            )
            gx_ref[tokens, cols] = grad_x.astype(BF16)
            gb_ref[tokens, cols_g] += dot(xw_ref[tokens, cols], ends[number], 1, 0)
            gc_ref[tokens, cols_g] += dot(dyw_ref[tokens, cols], starts[number], 1, 0)

    per_load = max(chunks // 4, 1)
    span_of_steps = LAG * (columns - 1)

    def exchange(s):
        f = s - forward_at
        b = s - backward_at

        @pl.when(jnp.logical_and(f >= 0, f < chunks))
        def _():
            forward(f)

        @pl.when(jnp.logical_and(b >= 0, b < chunks))
        def _():
            backward(b)

    for s in range(chunks + span_of_steps + WAIT):
        if s < chunks:
            if s % per_load == 0:
                loads[3 + 2 * (s // per_load)].wait()
                loads[4 + 2 * (s // per_load)].wait()
            summarize(s)
        if s < chunks + span_of_steps:
            exchange(s)
        if s < chunks:
            local(s)
        if s >= span_of_steps + WAIT:
            carried(s - span_of_steps - WAIT)
    gbc_ref[:, : groups * STATE] = gb_ref[...].astype(BF16)
    gbc_ref[:, groups * STATE :] = gc_ref[...].astype(BF16)

    def pair_copy(offset, c):
        slot = offset * pieces + c
        return pltpu.make_async_remote_copy(
            src_ref=pair_out.at[slot], dst_ref=pair_in.at[slot],
            send_sem=pair_send.at[slot], recv_sem=pair_recv.at[slot],
            device_id={"seq": k, "tp": mate}, device_id_type=MESH,
        )

    def chip_copy(offset, c):
        slot = (offset - 1) * pieces + c
        return pltpu.make_async_remote_copy(
            src_ref=chip_out.at[slot], dst_ref=chip_in.at[slot],
            send_sem=chip_send.at[slot], recv_sem=chip_recv.at[slot],
            device_id={"seq": k, "tp": owner_of(offset, True)}, device_id_type=MESH,
        )

    def partial(offset, same_core, c):
        for which in (0, 1):
            w_copy(offset, same_core, c, which).wait()
        slot = (offset * 2 + (1 if same_core else 0)) * pieces + c
        return dot(gbc_ref[...], w_all[slot], 1, 1)

    def give(offset, c):
        pair_out[offset * pieces + c] = partial(offset, False, c).astype(BF16)
        pair_copy(offset, c).start()

    def send_on(offset, c):
        own = partial(offset, True, c)
        pair_copy(offset, c).wait_recv()
        slot = offset * pieces + c
        chip_out[(offset - 1) * pieces + c] = (own + pair_in[slot].astype(F32)).astype(BF16)
        chip_copy(offset, c).start()

    for offset in range(1, chips):
        def body(s, carry):
            @pl.when(s < pieces)
            def _():
                give(offset, s)

            @pl.when(s >= 2)
            def _():
                send_on(offset, s - 2)

            return carry

        lax.fori_loop(0, pieces + 2, body, 0)

    def near_give(c, carry):
        give(0, c)
        return carry

    lax.fori_loop(0, pieces, near_give, 0)

    def final(c, carry):
        total = partial(0, True, c)
        pair_copy(0, c).wait_recv()
        total = total + pair_in[c].astype(F32)
        for offset in range(1, chips):
            chip_copy(offset, c).wait_recv()
            total = total + chip_in[(offset - 1) * pieces + c].astype(F32)
        cols = pl.ds(pl.multiple_of(c * piece, piece), piece)
        out_ref[:, cols] = total.astype(BF16)
        return carry

    lax.fori_loop(0, pieces, final, 0)

    def drain(c, carry):
        for offset in range(chips):
            pair_copy(offset, c).wait_send()
        for offset in range(1, chips):
            chip_copy(offset, c).wait_send()
        return carry

    lax.fori_loop(0, pieces, drain, 0)

    def drain_scan(c, carry):
        forward_drain(c)
        backward_drain(c)
        return carry

    lax.fori_loop(0, chunks, drain_scan, 0)

    @pl.when(sends_next)
    def _():
        to_next.wait_send()

    @pl.when(sends_prev)
    def _():
        to_prev.wait_send()


def per_device(inner_x, in_b, in_c, log_decay, doc_lengths, out_grad, w_b, w_c):
    tokens, inner = inner_x.shape
    heads = log_decay.shape[0]
    seq_count, tp_count = lax.axis_size("seq"), lax.axis_size("tp")
    block = w_b.shape[0] // tp_count
    chips = tp_count // 2
    piece = 256
    pieces = block // piece
    chunks = heads // 2
    wide = in_b.shape[1]
    groups = wide // STATE
    vmem = pltpu.VMEM
    dma = pltpu.SemaphoreType.DMA
    row = vmem((heads, 1, STATE), F32)
    square = lambda n: vmem((n, SPAN, SPAN), F32)
    return tuple(pl.pallas_call(
        functools.partial(fused_kernel, seq_count // 2, chips, pieces),
        out_shape=[
            vmem((tokens, inner), BF16),
            vmem((tokens, block), BF16),
        ],
        in_specs=[SMEM] + [ANY] * 7,
        out_specs=[pl.BlockSpec(memory_space=vmem)] * 2,
        scratch_shapes=[
            vmem((tokens, inner), BF16), vmem((tokens, inner), BF16),
            vmem((tokens, wide), BF16), vmem((tokens, wide), BF16),
            vmem((heads, tokens), F32),
            vmem((6, SPAN, heads), F32), vmem((2, heads, SPAN), F32),
            row, row, row,
            square(2), square(2 * groups), square(2 * groups),
            vmem((tokens, inner), BF16), vmem((tokens, inner), BF16),
            vmem((tokens, inner), F32),
            vmem((tokens, wide), F32), vmem((tokens, wide), F32), vmem((tokens, 2 * wide), BF16),
        ]
        + [vmem((inner, STATE), F32)] * 4
        + [vmem((inner, STATE), BF16)] * 6
        + [
            vmem((2 * chips * pieces, piece, 2 * wide), BF16),
            vmem((chips * pieces, tokens, piece), BF16),
            vmem((chips * pieces, tokens, piece), BF16),
            vmem(((chips - 1) * pieces, tokens, piece), BF16),
            vmem(((chips - 1) * pieces, tokens, piece), BF16),
            dma((11,)), dma((2, 2)), dma((4, chunks)), dma((4, chunks)),
            dma((2 * chips * pieces, 2)),
            dma((chips * pieces,)), dma((chips * pieces,)),
            dma(((chips - 1) * pieces,)), dma(((chips - 1) * pieces,)),
        ],
        compiler_params=pltpu.CompilerParams(
            collective_id=0, has_side_effects=True, vmem_limit_bytes=56 * 1024 * 1024
        ),
        name="fused",
    )(doc_lengths, inner_x, out_grad, in_b, in_c, log_decay, w_b, w_c))


def solution(mesh):
    placed = (
        P("seq", "tp"),
        P("seq", "tp"),
        P("seq", "tp"),
        P("tp", "seq"),
        P(),
        P("seq", "tp"),
        P(None, "tp"),
        P(None, "tp"),
    )
    return jax.shard_map(
        per_device,
        mesh=mesh,
        in_specs=placed,
        out_specs=(P("seq", "tp"), P("seq", "tp")),
        check_vma=False,
    )
```

```python
import functools

import jax
import jax.numpy as jnp
from jax import lax
from jax.experimental import pallas as pl
from jax.experimental.pallas import tpu as pltpu
from jax.sharding import PartitionSpec as P

HEAD_DIM = 64
STATE = 128
SPAN = 128
LAG = 5
WAIT = 6
F32 = jnp.float32
BF16 = jnp.bfloat16
MESH = pl.DeviceIdType.MESH
SMEM = pl.BlockSpec(memory_space=pltpu.SMEM)
ANY = pl.BlockSpec(memory_space=pl.ANY)


def dot(a, b, a_dim, b_dim):
    return lax.dot_general(a, b, (((a_dim,), (b_dim,)), ((), ())), preferred_element_type=F32)


def doc_of(lens_ref, position):
    end = 0
    doc = jnp.zeros_like(position)
    for k in range(lens_ref.shape[0] - 1):
        end = end + lens_ref[k]
        doc = doc + (position >= end).astype(jnp.int32)
    return doc


def span_decays(lens_ref, log_ref, number):
    heads, tokens = log_ref.shape
    first = lax.axis_index("seq") * tokens + number * SPAN
    cumulative = log_ref[:, number * SPAN : (number + 1) * SPAN]
    lane = lax.broadcasted_iota(jnp.int32, (heads, SPAN), 1)
    shift = 1
    while shift < SPAN:
        rolled = pltpu.roll(cumulative, shift, 1)
        cumulative = cumulative + jnp.where(lane >= shift, rolled, 0.0)
        shift *= 2
    doc_row = doc_of(lens_ref, first + lane)
    doc_last = doc_of(lens_ref, jnp.full((heads, SPAN), first + SPAN - 1, jnp.int32))
    before = jnp.full((heads, SPAN), first - 1, jnp.int32)
    doc_prior = jnp.where(before >= 0, doc_of(lens_ref, before), -1)
    last = jnp.broadcast_to(cumulative[:, SPAN - 1 :], (heads, SPAN))
    enter = jnp.where(doc_row == doc_prior, jnp.exp(cumulative), 0.0)
    leave = jnp.where(doc_row == doc_last, jnp.exp(last - cumulative), 0.0)
    total = jnp.where(doc_last == doc_prior, jnp.exp(last), 0.0)
    return cumulative, enter, leave, total


def fused_kernel(
    columns, chips, pieces, whole, lens_ref, x_hbm, dy_hbm, b_hbm, c_hbm, log_hbm, wb_ref, wc_ref, gx_ref, out_ref,
    x_ref, dy_ref, b_ref, c_ref, log_ref, turned, totals, d_ref, d_prev, d_next, bias, scores, mixed,
    xw_ref, dyw_ref, gx_local, gb_ref, gc_ref, gbc_ref, f0_ref, f_ref, g1_ref, g_ref,
    c_in, c_out, c_side, b_in, b_out, b_side,
    w_own, w_far, pair_out, pair_in, chip_out, chip_in,
    load_sems, d_sems, send_sems, recv_sems,
    w_sems, far_sems, pair_send, pair_recv, chip_send, chip_recv,
    *shared,
):
    summed = pieces - whole
    if whole:
        w_mate, w_cross, gbc_in, mate_sems, cross_sems, relay_sems, gbc_sems = shared
    heads = log_ref.shape[0]
    groups = b_ref.shape[1] // STATE
    chunks = heads // 2
    pairs = chunks // groups
    width = 2 * HEAD_DIM
    k = lax.axis_index("seq")
    m = k // 2
    r = k - 2 * m
    devices = 2 * columns
    partner = k + 1 - 2 * r
    t = lax.axis_index("tp")
    chip = t // 2
    core = t - 2 * chip
    mate = t + 1 - 2 * core
    block = out_ref.shape[1]
    piece = block // pieces
    depth = wb_ref.shape[1]
    z_at = m - 2 * (m // 2)
    z_mate = k + 2 - 4 * z_at
    here = 2 * z_at + r
    over_y = 2 * z_at + 1 - r
    over_z = 2 * (1 - z_at) + r
    across = 2 * (1 - z_at) + 1 - r

    def place(c):
        if not whole:
            return c
        held = c // 4
        pair_at = (c - 4 * held) // 2
        odd = c - 2 * (c // 2)
        added = (1 - pair_at) * (2 * across + odd) + pair_at * (2 * ((1 - odd) * over_y + odd * over_z) + 1)
        gathered = (1 - pair_at) * (2 * here + odd) + pair_at * 2 * ((1 - odd) * over_y + odd * over_z)
        return (1 - held) * added + held * gathered

    barrier = pltpu.get_barrier_semaphore()
    for offset in (-2, -1, 1, 2):
        @pl.when(jnp.logical_and(k + offset >= 0, k + offset < devices))
        def _():
            pl.semaphore_signal(
                barrier, inc=1, device_id={"seq": k + offset, "tp": t}, device_id_type=MESH
            )

    def owner_of(offset, same_core):
        at = lax.rem(chip + offset, chips)
        return 2 * at + (core if same_core else 1 - core)

    pl.semaphore_signal(barrier, inc=1, device_id={"seq": k, "tp": mate}, device_id_type=MESH)
    for offset in range(1, chips):
        pl.semaphore_signal(
            barrier, inc=1, device_id={"seq": k, "tp": owner_of(offset, True)}, device_id_type=MESH
        )
    if whole:
        pl.semaphore_signal(
            barrier, inc=1, device_id={"seq": k, "tp": owner_of(1, False)}, device_id_type=MESH
        )

    quarter = x_ref.shape[1] // 4
    loads = [
        pltpu.make_async_copy(log_hbm, log_ref, load_sems.at[0]),
        pltpu.make_async_copy(b_hbm, b_ref, load_sems.at[1]),
        pltpu.make_async_copy(c_hbm, c_ref, load_sems.at[2]),
    ]
    for q in range(4):
        cols = pl.ds(q * quarter, quarter)
        loads.append(pltpu.make_async_copy(x_hbm.at[:, cols], x_ref.at[:, cols], load_sems.at[3 + 2 * q]))
        loads.append(pltpu.make_async_copy(dy_hbm.at[:, cols], dy_ref.at[:, cols], load_sems.at[4 + 2 * q]))
    for load in loads:
        load.start()

    def rows_of(offset, same_core, c):
        at = owner_of(offset, same_core) * block + place(c) * piece
        return pl.ds(pl.multiple_of(at, piece), piece)

    def halves(which):
        return pl.ds(which * depth, depth)

    def far_slot(offset, same_core, c):
        return (2 * offset - (1 if offset else 0) + (1 if same_core else 0)) * summed + c

    def w_copy(offset, same_core, c, which):
        own = offset == 0 and same_core
        slot = c if own else far_slot(offset, same_core, c)
        return pltpu.make_async_copy(
            (wb_ref, wc_ref)[which].at[rows_of(offset, same_core, c)],
            (w_own if own else w_far).at[slot, :, halves(which)],
            (w_sems if own else far_sems).at[slot, which],
        )

    def mate_weights(g, which):
        return pltpu.make_async_remote_copy(
            src_ref=(wb_ref, wc_ref)[which].at[rows_of(0, False, summed + g)],
            dst_ref=w_mate.at[g, :, halves(which)],
            send_sem=mate_sems.at[0, g, which], recv_sem=mate_sems.at[1, g, which],
            device_id={"seq": k, "tp": mate}, device_id_type=MESH,
        )

    def cross_weights(g, same_core, which):
        source = 1 if same_core else 0
        return pltpu.make_async_remote_copy(
            src_ref=(wb_ref, wc_ref)[which].at[rows_of(1, same_core, summed + g)],
            dst_ref=w_cross.at[source, g, :, halves(which)],
            send_sem=cross_sems.at[0, source, g, which], recv_sem=cross_sems.at[1, source, g, which],
            device_id={"seq": k, "tp": owner_of(1, same_core)}, device_id_type=MESH,
        )

    def relay_weights(axis, source):
        return pltpu.make_async_remote_copy(
            src_ref=w_cross.at[source, 0], dst_ref=w_cross.at[source, 2 + axis],
            send_sem=relay_sems.at[0, axis, source], recv_sem=relay_sems.at[1, axis, source],
            device_id={"seq": z_mate if axis else partner, "tp": t}, device_id_type=MESH,
        )

    def group_columns(group, half):
        return pl.ds(half * groups * STATE + group * STATE, STATE)

    def gbc_copy(kind, group, half):
        cols = group_columns(group, half)
        source = gbc_in.at[1] if kind == 2 else gbc_ref
        return pltpu.make_async_remote_copy(
            src_ref=source.at[:, cols], dst_ref=gbc_in.at[kind, :, cols],
            send_sem=gbc_sems.at[0, kind, group, half], recv_sem=gbc_sems.at[1, kind, group, half],
            device_id={"seq": k, "tp": owner_of(1, True) if kind == 1 else mate}, device_id_type=MESH,
        )

    for offset in range(chips):
        for same_core in (False, True):
            def fetch(c, carry):
                for which in (0, 1):
                    w_copy(offset, same_core, c, which).start()
                return carry

            lax.fori_loop(0, pieces if offset == 0 and same_core else summed, fetch, 0)

    loads[0].wait()
    low = lax.broadcasted_iota(jnp.int32, (SPAN, width), 1) < HEAD_DIM
    low_mask = low.astype(F32).astype(BF16)
    high_mask = (1.0 - low.astype(F32)).astype(BF16)
    row_id = lax.broadcasted_iota(jnp.int32, (SPAN, SPAN), 0)
    col_id = lax.broadcasted_iota(jnp.int32, (SPAN, SPAN), 1)
    for number in range(2):
        cumulative, enter, leave, total = span_decays(lens_ref, log_ref, number)
        log_ref[:, number * SPAN : (number + 1) * SPAN] = cumulative
        turned[3 * number] = jnp.transpose(cumulative)
        turned[3 * number + 1] = jnp.transpose(enter)
        turned[3 * number + 2] = jnp.transpose(leave)
        totals[number] = total
        first = k * log_ref.shape[1] + number * SPAN
        same = jnp.logical_and(
            doc_of(lens_ref, first + row_id) == doc_of(lens_ref, first + col_id), row_id >= col_id
        )
        bias[number] = jnp.where(same, 0.0, -1e30)
    both = totals[0] * totals[1]
    for h in range(heads):
        d_ref[h] = both[h : h + 1, :]

    count = jnp.minimum(k, 2) + jnp.minimum(devices - 1 - k, 2) + chips + (1 if whole else 0)
    pl.semaphore_wait(barrier, count)

    def copy(stream, c, source, target, to):
        rows = pl.ds(pl.multiple_of(c * width, width), width)
        return pltpu.make_async_remote_copy(
            src_ref=source.at[rows], dst_ref=target.at[rows],
            send_sem=send_sems.at[stream, c], recv_sem=recv_sems.at[stream, c],
            device_id={"seq": to, "tp": t}, device_id_type=MESH,
        )

    def decay_copy(stream, target, to):
        return pltpu.make_async_remote_copy(
            src_ref=d_ref, dst_ref=target,
            send_sem=d_sems.at[0, stream], recv_sem=d_sems.at[1, stream],
            device_id={"seq": to, "tp": t}, device_id_type=MESH,
        )

    to_next = decay_copy(0, d_prev, k + 1)
    to_prev = decay_copy(1, d_next, k - 1)
    sends_next = jnp.logical_and(k + 1 >= 2, k + 1 < devices)
    sends_prev = jnp.logical_and(k >= 1, k - 1 <= devices - 3)

    @pl.when(sends_next)
    def _():
        to_next.start()

    @pl.when(sends_prev)
    def _():
        to_prev.start()

    if whole:
        for g in range(2):
            for which in (0, 1):
                for same_core in (False, True):
                    cross_weights(g, same_core, which).start()
        for g in range(whole):
            for which in (0, 1):
                mate_weights(g, which).start()

    loads[1].wait()
    loads[2].wait()

    def spans(number):
        return slice(number * SPAN, (number + 1) * SPAN)

    def spread(kind, number, pair):
        held = turned.at[3 * number + kind]
        one = jnp.broadcast_to(held[:, 2 * pair : 2 * pair + 1], (SPAN, width))
        two = jnp.broadcast_to(held[:, 2 * pair + 1 : 2 * pair + 2], (SPAN, width))
        return jnp.where(low, one, two)

    def by_head(number, pair):
        return jnp.concatenate(
            [
                jnp.broadcast_to(totals[number, h : h + 1, :], (HEAD_DIM, STATE))
                for h in (2 * pair, 2 * pair + 1)
            ],
            axis=0,
        )

    def summarize(pair):
        group = pair // pairs
        cols = slice(pair * width, (pair + 1) * width)
        cols_g = slice(group * STATE, (group + 1) * STATE)
        states, grads = [], []
        for number in (0, 1):
            tokens = spans(number)
            x_weighted = (x_ref[tokens, cols].astype(F32) * spread(2, number, pair)).astype(BF16)
            dy_weighted = (dy_ref[tokens, cols].astype(F32) * spread(1, number, pair)).astype(BF16)
            xw_ref[tokens, cols] = x_weighted
            dyw_ref[tokens, cols] = dy_weighted
            states.append(dot(x_weighted, b_ref[tokens, cols_g], 0, 0))
            grads.append(dot(dy_weighted, c_ref[tokens, cols_g], 0, 0))
        f0_ref[cols] = states[0]
        f_ref[cols] = states[1] + by_head(1, pair) * states[0]
        g1_ref[cols] = grads[1]
        g_ref[cols] = grads[0] + by_head(0, pair) * grads[1]

    def local(pair):
        group = pair // pairs
        cols = slice(pair * width, (pair + 1) * width)
        cols_g = slice(group * STATE, (group + 1) * STATE)
        for number in (0, 1):
            tokens = spans(number)
            slot = 2 * group + number
            if pair == group * pairs:
                scores[slot] = dot(c_ref[tokens, cols_g], b_ref[tokens, cols_g], 1, 1)
            x_part, dy_part = x_ref[tokens, cols], dy_ref[tokens, cols]
            x_blocks = jnp.concatenate([x_part * low_mask, x_part * high_mask], axis=0)
            dy_blocks = jnp.concatenate([dy_part * low_mask, dy_part * high_mask], axis=0)
            dots = dot(dy_part, x_blocks, 1, 1)
            score_low = []
            added = None
            for e in range(2):
                h = 2 * pair + e
                column = jnp.broadcast_to(turned[3 * number, :, h : h + 1], (SPAN, SPAN))
                gap = column - log_ref[h : h + 1, number * SPAN : (number + 1) * SPAN]
                within = jnp.exp(gap + bias[number])
                term = within * dots[:, e * SPAN : (e + 1) * SPAN]
                added = term if added is None else added + term
                score_low.append((within * scores[slot]).astype(BF16))
            mixed[slot] = added if pair == group * pairs else mixed[slot] + added
            gx_local[tokens, cols] = dot(jnp.concatenate(score_low, axis=0), dy_blocks, 0, 0)
            if pair == group * pairs + pairs - 1:
                mixed_low = mixed[slot].astype(BF16)
                gb_ref[tokens, cols_g] = dot(mixed_low, c_ref[tokens, cols_g], 0, 0)
                gc_ref[tokens, cols_g] = dot(mixed_low, b_ref[tokens, cols_g], 1, 0)

    def stream(base, has_in, has_next, ahead, source, buf_in, buf_out, buf_side, near, arrival, passes_own):
        chain = lambda c: copy(base, c, buf_out, buf_in, ahead)
        side_own = lambda c: copy(base + 1, c, buf_out, buf_side, partner)
        side_in = lambda c: copy(base + 1, c, buf_in, buf_side, partner)
        passes_in = jnp.logical_and(jnp.logical_not(passes_own), has_in)
        side_arrives = jnp.logical_or(jnp.logical_not(passes_own), has_in)

        def step(c):
            @pl.when(jnp.logical_and(has_in, c == 0))
            def _():
                arrival.wait_recv()

            @pl.when(has_in)
            def _():
                chain(c).wait_recv()

                @pl.when(jnp.logical_not(passes_own))
                def _():
                    side_in(c).start()

                for e in range(2):
                    h = 2 * c + e
                    rows = pl.ds(pl.multiple_of(h * HEAD_DIM, HEAD_DIM), HEAD_DIM)
                    product = d_ref[h] * near[h]
                    buf_out[rows, :] = (source[rows, :] + product * buf_in[rows, :].astype(F32)).astype(BF16)

            @pl.when(jnp.logical_not(has_in))
            def _():
                rows = pl.ds(pl.multiple_of(c * width, width), width)
                buf_out[rows, :] = source[rows, :].astype(BF16)

            @pl.when(passes_own)
            def _():
                side_own(c).start()

            @pl.when(has_next)
            def _():
                chain(c).start()

        def finish(c):
            @pl.when(side_arrives)
            def _():
                side_own(c).wait_recv()

            for e in range(2):
                h = 2 * c + e
                rows = slice(h * HEAD_DIM, (h + 1) * HEAD_DIM)

                @pl.when(has_in)
                def _():
                    source[rows, :] = (
                        buf_side[rows, :].astype(F32) + near[h] * buf_in[rows, :].astype(F32)
                    )

                @pl.when(jnp.logical_and(jnp.logical_not(has_in), side_arrives))
                def _():
                    source[rows, :] = buf_side[rows, :].astype(F32)

                @pl.when(jnp.logical_not(side_arrives))
                def _():
                    source[rows, :] = jnp.zeros((HEAD_DIM, STATE), F32)

        def drain(c):
            @pl.when(has_next)
            def _():
                chain(c).wait_send()

            @pl.when(jnp.logical_or(passes_own, passes_in))
            def _():
                side_own(c).wait_send()

        return step, finish, drain

    forward, forward_end, forward_drain = stream(
        0, m > 0, m < columns - 1, k + 2, f_ref, c_in, c_out, c_side, d_prev, to_next, r == 0
    )
    backward, backward_end, backward_drain = stream(
        2, m < columns - 1, m > 0, k - 2, g_ref, b_in, b_out, b_side, d_next, to_prev, r == 1
    )
    lead = LAG * (columns - 1 - 2 * m)
    forward_at = jnp.maximum(-lead, 0)
    backward_at = jnp.maximum(lead, 0)

    def carried(pair):
        group = pair // pairs
        cols = slice(pair * width, (pair + 1) * width)
        cols_g = slice(group * STATE, (group + 1) * STATE)
        forward_end(pair)
        backward_end(pair)
        arrived, ended = f_ref[cols], g_ref[cols]
        starts = [arrived.astype(BF16), (f0_ref[cols] + by_head(0, pair) * arrived).astype(BF16)]
        ends = [(g1_ref[cols] + by_head(1, pair) * ended).astype(BF16), ended.astype(BF16)]
        for number in (0, 1):
            tokens = spans(number)
            grad_x = gx_local[tokens, cols] + spread(2, number, pair) * dot(
                b_ref[tokens, cols_g], ends[number], 1, 1
            )
            gx_ref[tokens, cols] = grad_x.astype(BF16)
            gb_ref[tokens, cols_g] += dot(xw_ref[tokens, cols], ends[number], 1, 0)
            gc_ref[tokens, cols_g] += dot(dyw_ref[tokens, cols], starts[number], 1, 0)
        if pair == group * pairs + pairs - 1:
            for half in (0, 1):
                at = (half * groups + group) * STATE
                gbc_ref[:, at : at + STATE] = (gc_ref if half else gb_ref)[:, cols_g].astype(BF16)
                if whole:
                    gbc_copy(1, group, half).start()
                    gbc_copy(0, group, half).start()

    per_load = max(chunks // 4, 1)
    span_of_steps = LAG * (columns - 1)

    def exchange(s):
        f = s - forward_at
        b = s - backward_at

        @pl.when(jnp.logical_and(f >= 0, f < chunks))
        def _():
            forward(f)

        @pl.when(jnp.logical_and(b >= 0, b < chunks))
        def _():
            backward(b)

    for s in range(chunks + span_of_steps + WAIT):
        if s < chunks:
            if s % per_load == 0:
                loads[3 + 2 * (s // per_load)].wait()
                loads[4 + 2 * (s // per_load)].wait()
            summarize(s)
        if s < chunks + span_of_steps:
            exchange(s)
        if s < chunks:
            local(s)
        if s >= span_of_steps + WAIT:
            carried(s - span_of_steps - WAIT)

    def relay_group(group):
        for half in (0, 1):
            gbc_copy(1, group, half).wait_recv()
            gbc_copy(2, group, half).start()

    if whole:
        for source in (0, 1):
            for which in (0, 1):
                cross_weights(0, source == 1, which).wait_recv()
            for axis in (0, 1):
                relay_weights(axis, source).start()
        for group in range(groups - 1):
            relay_group(group)

    def pair_copy(offset, c):
        slot = offset * summed + c
        return pltpu.make_async_remote_copy(
            src_ref=pair_out.at[slot], dst_ref=pair_in.at[slot],
            send_sem=pair_send.at[slot], recv_sem=pair_recv.at[slot],
            device_id={"seq": k, "tp": mate}, device_id_type=MESH,
        )

    def chip_copy(offset, c):
        slot = (offset - 1) * summed + c
        return pltpu.make_async_remote_copy(
            src_ref=chip_out.at[slot], dst_ref=chip_in.at[slot],
            send_sem=chip_send.at[slot], recv_sem=chip_recv.at[slot],
            device_id={"seq": k, "tp": owner_of(offset, True)}, device_id_type=MESH,
        )

    def partial(offset, same_core, c):
        for which in (0, 1):
            w_copy(offset, same_core, c, which).wait()
        weights = w_own[c] if offset == 0 and same_core else w_far[far_slot(offset, same_core, c)]
        return dot(gbc_ref[...], weights, 1, 1)

    def give(offset, c):
        pair_out[offset * summed + c] = partial(offset, False, c).astype(BF16)
        pair_copy(offset, c).start()

    def send_on(offset, c):
        own = partial(offset, True, c)
        pair_copy(offset, c).wait_recv()
        slot = offset * summed + c
        chip_out[(offset - 1) * summed + c] = (own + pair_in[slot].astype(F32)).astype(BF16)
        chip_copy(offset, c).start()

    for offset in range(1, chips):
        def body(s, carry):
            @pl.when(s < summed)
            def _():
                give(offset, s)

            @pl.when(s >= 2)
            def _():
                send_on(offset, s - 2)

            return carry

        lax.fori_loop(0, summed + 2, body, 0)

    def near_give(c, carry):
        give(0, c)
        return carry

    lax.fori_loop(0, summed, near_give, 0)

    def gather(g, carry):
        for which in (0, 1):
            w_copy(0, True, summed + g, which).wait()
            mate_weights(g, which).wait_recv()
        total = dot(gbc_ref[...], w_own[summed + g], 1, 1) + dot(gbc_in[0], w_mate[g], 1, 1)
        total = total + dot(gbc_in[1], w_cross[1, g], 1, 1) + dot(gbc_in[2], w_cross[0, g], 1, 1)
        cols = pl.ds(pl.multiple_of(place(summed + g) * piece, piece), piece)
        out_ref[:, cols] = total.astype(BF16)
        return carry

    if whole:
        relay_group(groups - 1)
        for which in (0, 1):
            for source in (0, 1):
                cross_weights(1, source == 1, which).wait_recv()
        for group in range(groups):
            for half in (0, 1):
                gbc_copy(0, group, half).wait_recv()
                gbc_copy(2, group, half).wait_recv()
        lax.fori_loop(0, 2, gather, 0)

    def final(c, carry):
        total = partial(0, True, c)
        pair_copy(0, c).wait_recv()
        total = total + pair_in[c].astype(F32)
        for offset in range(1, chips):
            chip_copy(offset, c).wait_recv()
            total = total + chip_in[(offset - 1) * summed + c].astype(F32)
        cols = pl.ds(pl.multiple_of(place(c) * piece, piece), piece)
        out_ref[:, cols] = total.astype(BF16)
        return carry

    early = summed - 1 if whole else summed
    lax.fori_loop(0, early, final, 0)
    if whole:
        for axis in (0, 1):
            for source in (0, 1):
                relay_weights(axis, source).wait_recv()
        lax.fori_loop(2, whole, gather, 0)
        final(early, 0)

    def drain(c, carry):
        for offset in range(chips):
            pair_copy(offset, c).wait_send()
        for offset in range(1, chips):
            chip_copy(offset, c).wait_send()
        return carry

    lax.fori_loop(0, summed, drain, 0)

    if whole:
        for which in (0, 1):
            for g in range(2):
                for same_core in (False, True):
                    cross_weights(g, same_core, which).wait_send()
            for g in range(whole):
                mate_weights(g, which).wait_send()
        for axis in (0, 1):
            for source in (0, 1):
                relay_weights(axis, source).wait_send()
        for kind in range(3):
            for group in range(groups):
                for half in (0, 1):
                    gbc_copy(kind, group, half).wait_send()

    def drain_scan(c, carry):
        forward_drain(c)
        backward_drain(c)
        return carry

    lax.fori_loop(0, chunks, drain_scan, 0)

    @pl.when(sends_next)
    def _():
        to_next.wait_send()

    @pl.when(sends_prev)
    def _():
        to_prev.wait_send()


def per_device(inner_x, in_b, in_c, log_decay, doc_lengths, out_grad, w_b, w_c):
    tokens, inner = inner_x.shape
    heads = log_decay.shape[0]
    seq_count, tp_count = lax.axis_size("seq"), lax.axis_size("tp")
    block = w_b.shape[0] // tp_count
    chips = tp_count // 2
    piece = 256
    pieces = block // piece
    chunks = heads // 2
    wide = in_b.shape[1]
    whole = 4 if chips == 2 and pieces == 8 and seq_count % 4 == 0 else 0
    summed = pieces - whole
    groups = wide // STATE
    vmem = pltpu.VMEM
    dma = pltpu.SemaphoreType.DMA
    row = vmem((heads, 1, STATE), F32)
    square = lambda n: vmem((n, SPAN, SPAN), F32)
    return tuple(pl.pallas_call(
        functools.partial(fused_kernel, seq_count // 2, chips, pieces, whole),
        out_shape=[
            vmem((tokens, inner), BF16),
            vmem((tokens, block), BF16),
        ],
        in_specs=[SMEM] + [ANY] * 7,
        out_specs=[pl.BlockSpec(memory_space=vmem)] * 2,
        scratch_shapes=[
            vmem((tokens, inner), BF16), vmem((tokens, inner), BF16),
            vmem((tokens, wide), BF16), vmem((tokens, wide), BF16),
            vmem((heads, tokens), F32),
            vmem((6, SPAN, heads), F32), vmem((2, heads, SPAN), F32),
            row, row, row,
            square(2), square(2 * groups), square(2 * groups),
            vmem((tokens, inner), BF16), vmem((tokens, inner), BF16),
            vmem((tokens, inner), F32),
            vmem((tokens, wide), F32), vmem((tokens, wide), F32), vmem((tokens, 2 * wide), BF16),
        ]
        + [vmem((inner, STATE), F32)] * 4
        + [vmem((inner, STATE), BF16)] * 6
        + [
            vmem((pieces, piece, 2 * wide), BF16),
            vmem(((2 * chips - 1) * summed, piece, 2 * wide), BF16),
            vmem((chips * summed, tokens, piece), BF16),
            vmem((chips * summed, tokens, piece), BF16),
            vmem(((chips - 1) * summed, tokens, piece), BF16),
            vmem(((chips - 1) * summed, tokens, piece), BF16),
            dma((11,)), dma((2, 2)), dma((4, chunks)), dma((4, chunks)),
            dma((pieces, 2)), dma(((2 * chips - 1) * summed, 2)),
            dma((chips * summed,)), dma((chips * summed,)),
            dma(((chips - 1) * summed,)), dma(((chips - 1) * summed,)),
        ]
        + ([
            vmem((whole, piece, 2 * wide), BF16),
            vmem((2, whole, piece, 2 * wide), BF16),
            vmem((3, tokens, 2 * wide), BF16),
            dma((2, whole, 2)), dma((2, 2, 2, 2)), dma((2, 2, 2)), dma((2, 3, groups, 2)),
        ] if whole else []),
        compiler_params=pltpu.CompilerParams(
            collective_id=0, has_side_effects=True, vmem_limit_bytes=56 * 1024 * 1024
        ),
        name="fused",
    )(doc_lengths, inner_x, out_grad, in_b, in_c, log_decay, w_b, w_c))


def solution(mesh):
    placed = (
        P("seq", "tp"),
        P("seq", "tp"),
        P("seq", "tp"),
        P("tp", "seq"),
        P(),
        P("seq", "tp"),
        P(None, "tp"),
        P(None, "tp"),
    )
    return jax.shard_map(
        per_device,
        mesh=mesh,
        in_specs=placed,
        out_specs=(P("seq", "tp"), P("seq", "tp")),
        check_vma=False,
    )
```

```python
import functools

import jax
import jax.numpy as jnp
from jax import lax
from jax.experimental import pallas as pl
from jax.experimental.pallas import tpu as pltpu
from jax.sharding import PartitionSpec as P

HEAD_DIM = 64
STATE = 128
SPAN = 128
LAG = 5
WAIT = 6
F32 = jnp.float32
BF16 = jnp.bfloat16
MESH = pl.DeviceIdType.MESH
SMEM = pl.BlockSpec(memory_space=pltpu.SMEM)
ANY = pl.BlockSpec(memory_space=pl.ANY)


def dot(a, b, a_dim, b_dim):
    return lax.dot_general(a, b, (((a_dim,), (b_dim,)), ((), ())), preferred_element_type=F32)


def doc_of(lens_ref, position):
    end = 0
    doc = jnp.zeros_like(position)
    for k in range(lens_ref.shape[0] - 1):
        end = end + lens_ref[k]
        doc = doc + (position >= end).astype(jnp.int32)
    return doc


def span_decays(lens_ref, log_ref, number):
    heads, tokens = log_ref.shape
    first = lax.axis_index("seq") * tokens + number * SPAN
    cumulative = log_ref[:, number * SPAN : (number + 1) * SPAN]
    lane = lax.broadcasted_iota(jnp.int32, (heads, SPAN), 1)
    shift = 1
    while shift < SPAN:
        rolled = pltpu.roll(cumulative, shift, 1)
        cumulative = cumulative + jnp.where(lane >= shift, rolled, 0.0)
        shift *= 2
    doc_row = doc_of(lens_ref, first + lane)
    doc_last = doc_of(lens_ref, jnp.full((heads, SPAN), first + SPAN - 1, jnp.int32))
    before = jnp.full((heads, SPAN), first - 1, jnp.int32)
    doc_prior = jnp.where(before >= 0, doc_of(lens_ref, before), -1)
    last = jnp.broadcast_to(cumulative[:, SPAN - 1 :], (heads, SPAN))
    enter = jnp.where(doc_row == doc_prior, jnp.exp(cumulative), 0.0)
    leave = jnp.where(doc_row == doc_last, jnp.exp(last - cumulative), 0.0)
    total = jnp.where(doc_last == doc_prior, jnp.exp(last), 0.0)
    return cumulative, enter, leave, total


def fused_kernel(
    columns, chips, pieces, whole, lens_ref, x_hbm, dy_hbm, b_hbm, c_hbm, log_hbm, wb_ref, wc_ref, gx_ref, out_ref,
    x_ref, dy_ref, b_ref, c_ref, log_ref, turned, totals, d_ref, d_prev, d_next, bias, scores, mixed,
    xw_ref, dyw_ref, gx_local, gb_ref, gc_ref, gbc_ref, f0_ref, f_ref, g1_ref, g_ref,
    c_in, c_out, c_side, b_in, b_out, b_side,
    w_own, w_far, pair_out, pair_in, chip_out, chip_in,
    load_sems, d_sems, send_sems, recv_sems,
    w_sems, pair_send, pair_recv, chip_send, chip_recv,
    *shared,
):
    summed = pieces - whole
    if whole:
        w_mate, w_cross, gbc_in, mate_sems, cross_sems, relay_sems, gbc_sems = shared
    heads = log_ref.shape[0]
    groups = b_ref.shape[1] // STATE
    chunks = heads // 2
    pairs = chunks // groups
    width = 2 * HEAD_DIM
    k = lax.axis_index("seq")
    m = k // 2
    r = k - 2 * m
    devices = 2 * columns
    partner = k + 1 - 2 * r
    t = lax.axis_index("tp")
    chip = t // 2
    core = t - 2 * chip
    mate = t + 1 - 2 * core
    block = out_ref.shape[1]
    piece = block // pieces
    depth = wb_ref.shape[1]
    z_at = m - 2 * (m // 2)
    z_mate = k + 2 - 4 * z_at
    here = 2 * z_at + r
    over_y = 2 * z_at + 1 - r
    over_z = 2 * (1 - z_at) + r
    across = 2 * (1 - z_at) + 1 - r

    def place(c):
        if not whole:
            return c
        held = c // 4
        pair_at = (c - 4 * held) // 2
        odd = c - 2 * (c // 2)
        added = (1 - pair_at) * (2 * across + odd) + pair_at * (2 * ((1 - odd) * over_y + odd * over_z) + 1)
        gathered = (1 - pair_at) * (2 * here + odd) + pair_at * 2 * ((1 - odd) * over_y + odd * over_z)
        return (1 - held) * added + held * gathered

    barrier = pltpu.get_barrier_semaphore()
    for offset in (-2, -1, 1, 2):
        @pl.when(jnp.logical_and(k + offset >= 0, k + offset < devices))
        def _():
            pl.semaphore_signal(
                barrier, inc=1, device_id={"seq": k + offset, "tp": t}, device_id_type=MESH
            )

    def owner_of(offset, same_core):
        at = lax.rem(chip + offset, chips)
        return 2 * at + (core if same_core else 1 - core)

    pl.semaphore_signal(barrier, inc=1, device_id={"seq": k, "tp": mate}, device_id_type=MESH)
    for offset in range(1, chips):
        pl.semaphore_signal(
            barrier, inc=1, device_id={"seq": k, "tp": owner_of(offset, True)}, device_id_type=MESH
        )
    if whole:
        pl.semaphore_signal(
            barrier, inc=1, device_id={"seq": k, "tp": owner_of(1, False)}, device_id_type=MESH
        )

    quarter = x_ref.shape[1] // 4
    loads = [
        pltpu.make_async_copy(log_hbm, log_ref, load_sems.at[0]),
        pltpu.make_async_copy(b_hbm, b_ref, load_sems.at[1]),
        pltpu.make_async_copy(c_hbm, c_ref, load_sems.at[2]),
    ]
    for q in range(4):
        cols = pl.ds(q * quarter, quarter)
        loads.append(pltpu.make_async_copy(x_hbm.at[:, cols], x_ref.at[:, cols], load_sems.at[3 + 2 * q]))
        loads.append(pltpu.make_async_copy(dy_hbm.at[:, cols], dy_ref.at[:, cols], load_sems.at[4 + 2 * q]))
    for load in loads:
        load.start()

    def rows_of(offset, same_core, c):
        at = owner_of(offset, same_core) * block + place(c) * piece
        return pl.ds(pl.multiple_of(at, piece), piece)

    def halves(which):
        return pl.ds(which * depth, depth)

    def far_slot(offset, same_core, c):
        return (2 * offset - (1 if offset else 0) + (1 if same_core else 0)) * summed + c

    def w_copy(offset, same_core, c, which):
        own = offset == 0 and same_core
        slot = c if own else far_slot(offset, same_core, c)
        return pltpu.make_async_copy(
            (wb_ref, wc_ref)[which].at[rows_of(offset, same_core, c)],
            (w_own if own else w_far).at[slot, :, halves(which)],
            w_sems.at[0 if own else 1],
        )

    def mate_weights(g, which):
        return pltpu.make_async_remote_copy(
            src_ref=(wb_ref, wc_ref)[which].at[rows_of(0, False, summed + g)],
            dst_ref=w_mate.at[g, :, halves(which)],
            send_sem=mate_sems.at[0], recv_sem=mate_sems.at[1],
            device_id={"seq": k, "tp": mate}, device_id_type=MESH,
        )

    def cross_weights(g, same_core, which):
        source = 1 if same_core else 0
        return pltpu.make_async_remote_copy(
            src_ref=(wb_ref, wc_ref)[which].at[rows_of(1, same_core, summed + g)],
            dst_ref=w_cross.at[source, g, :, halves(which)],
            send_sem=cross_sems.at[0], recv_sem=cross_sems.at[1 + g],
            device_id={"seq": k, "tp": owner_of(1, same_core)}, device_id_type=MESH,
        )

    def relay_weights(axis, source):
        return pltpu.make_async_remote_copy(
            src_ref=w_cross.at[source, 0], dst_ref=w_cross.at[source, 2 + axis],
            send_sem=relay_sems.at[0], recv_sem=relay_sems.at[1 + axis],
            device_id={"seq": z_mate if axis else partner, "tp": t}, device_id_type=MESH,
        )

    def group_columns(group, half):
        return pl.ds(half * groups * STATE + group * STATE, STATE)

    def gbc_copy(kind, group, half):
        cols = group_columns(group, half)
        source = gbc_in.at[1] if kind == 2 else gbc_ref
        return pltpu.make_async_remote_copy(
            src_ref=source.at[:, cols], dst_ref=gbc_in.at[kind, :, cols],
            send_sem=gbc_sems.at[0], recv_sem=gbc_sems.at[3 + group if kind == 1 else 1 + kind // 2],
            device_id={"seq": k, "tp": owner_of(1, True) if kind == 1 else mate}, device_id_type=MESH,
        )

    for offset in range(chips):
        for same_core in (False, True):
            def fetch(c, carry):
                for which in (0, 1):
                    w_copy(offset, same_core, c, which).start()
                return carry

            lax.fori_loop(0, pieces if offset == 0 and same_core else summed, fetch, 0)

    loads[0].wait()
    low = lax.broadcasted_iota(jnp.int32, (SPAN, width), 1) < HEAD_DIM
    low_mask = low.astype(F32).astype(BF16)
    high_mask = (1.0 - low.astype(F32)).astype(BF16)
    row_id = lax.broadcasted_iota(jnp.int32, (SPAN, SPAN), 0)
    col_id = lax.broadcasted_iota(jnp.int32, (SPAN, SPAN), 1)
    for number in range(2):
        cumulative, enter, leave, total = span_decays(lens_ref, log_ref, number)
        log_ref[:, number * SPAN : (number + 1) * SPAN] = cumulative
        turned[3 * number] = jnp.transpose(cumulative)
        turned[3 * number + 1] = jnp.transpose(enter)
        turned[3 * number + 2] = jnp.transpose(leave)
        totals[number] = total
        first = k * log_ref.shape[1] + number * SPAN
        same = jnp.logical_and(
            doc_of(lens_ref, first + row_id) == doc_of(lens_ref, first + col_id), row_id >= col_id
        )
        bias[number] = jnp.where(same, 0.0, -1e30)
    both = totals[0] * totals[1]
    for h in range(heads):
        d_ref[h] = both[h : h + 1, :]

    count = jnp.minimum(k, 2) + jnp.minimum(devices - 1 - k, 2) + chips + (1 if whole else 0)
    pl.semaphore_wait(barrier, count)

    def copy(stream, c, source, target, to):
        rows = pl.ds(pl.multiple_of(c * width, width), width)
        return pltpu.make_async_remote_copy(
            src_ref=source.at[rows], dst_ref=target.at[rows],
            send_sem=send_sems.at[stream], recv_sem=recv_sems.at[stream, c],
            device_id={"seq": to, "tp": t}, device_id_type=MESH,
        )

    def settle(held, sem):
        pltpu.make_async_copy(held, held, sem).wait()

    def decay_copy(stream, target, to):
        return pltpu.make_async_remote_copy(
            src_ref=d_ref, dst_ref=target,
            send_sem=d_sems.at[0, stream], recv_sem=d_sems.at[1, stream],
            device_id={"seq": to, "tp": t}, device_id_type=MESH,
        )

    to_next = decay_copy(0, d_prev, k + 1)
    to_prev = decay_copy(1, d_next, k - 1)
    sends_next = jnp.logical_and(k + 1 >= 2, k + 1 < devices)
    sends_prev = jnp.logical_and(k >= 1, k - 1 <= devices - 3)

    @pl.when(sends_next)
    def _():
        to_next.start()

    @pl.when(sends_prev)
    def _():
        to_prev.start()

    if whole:
        for g in range(2):
            for which in (0, 1):
                for same_core in (False, True):
                    cross_weights(g, same_core, which).start()
        for g in range(whole):
            for which in (0, 1):
                mate_weights(g, which).start()

    loads[1].wait()
    loads[2].wait()

    def spans(number):
        return slice(number * SPAN, (number + 1) * SPAN)

    def spread(kind, number, pair):
        held = turned.at[3 * number + kind]
        one = jnp.broadcast_to(held[:, 2 * pair : 2 * pair + 1], (SPAN, width))
        two = jnp.broadcast_to(held[:, 2 * pair + 1 : 2 * pair + 2], (SPAN, width))
        return jnp.where(low, one, two)

    def by_head(number, pair):
        return jnp.concatenate(
            [
                jnp.broadcast_to(totals[number, h : h + 1, :], (HEAD_DIM, STATE))
                for h in (2 * pair, 2 * pair + 1)
            ],
            axis=0,
        )

    def summarize(pair):
        group = pair // pairs
        cols = slice(pair * width, (pair + 1) * width)
        cols_g = slice(group * STATE, (group + 1) * STATE)
        states, grads = [], []
        for number in (0, 1):
            tokens = spans(number)
            x_weighted = (x_ref[tokens, cols].astype(F32) * spread(2, number, pair)).astype(BF16)
            dy_weighted = (dy_ref[tokens, cols].astype(F32) * spread(1, number, pair)).astype(BF16)
            xw_ref[tokens, cols] = x_weighted
            dyw_ref[tokens, cols] = dy_weighted
            states.append(dot(x_weighted, b_ref[tokens, cols_g], 0, 0))
            grads.append(dot(dy_weighted, c_ref[tokens, cols_g], 0, 0))
        f0_ref[cols] = states[0]
        f_ref[cols] = states[1] + by_head(1, pair) * states[0]
        g1_ref[cols] = grads[1]
        g_ref[cols] = grads[0] + by_head(0, pair) * grads[1]

    def local(pair):
        group = pair // pairs
        cols = slice(pair * width, (pair + 1) * width)
        cols_g = slice(group * STATE, (group + 1) * STATE)
        for number in (0, 1):
            tokens = spans(number)
            slot = 2 * group + number
            if pair == group * pairs:
                scores[slot] = dot(c_ref[tokens, cols_g], b_ref[tokens, cols_g], 1, 1)
            x_part, dy_part = x_ref[tokens, cols], dy_ref[tokens, cols]
            x_blocks = jnp.concatenate([x_part * low_mask, x_part * high_mask], axis=0)
            dy_blocks = jnp.concatenate([dy_part * low_mask, dy_part * high_mask], axis=0)
            dots = dot(dy_part, x_blocks, 1, 1)
            score_low = []
            added = None
            for e in range(2):
                h = 2 * pair + e
                column = jnp.broadcast_to(turned[3 * number, :, h : h + 1], (SPAN, SPAN))
                gap = column - log_ref[h : h + 1, number * SPAN : (number + 1) * SPAN]
                within = jnp.exp(gap + bias[number])
                term = within * dots[:, e * SPAN : (e + 1) * SPAN]
                added = term if added is None else added + term
                score_low.append((within * scores[slot]).astype(BF16))
            mixed[slot] = added if pair == group * pairs else mixed[slot] + added
            gx_local[tokens, cols] = dot(jnp.concatenate(score_low, axis=0), dy_blocks, 0, 0)
            if pair == group * pairs + pairs - 1:
                mixed_low = mixed[slot].astype(BF16)
                gb_ref[tokens, cols_g] = dot(mixed_low, c_ref[tokens, cols_g], 0, 0)
                gc_ref[tokens, cols_g] = dot(mixed_low, b_ref[tokens, cols_g], 1, 0)

    def stream(base, has_in, has_next, ahead, source, buf_in, buf_out, buf_side, near, arrival, passes_own):
        chain = lambda c: copy(base, c, buf_out, buf_in, ahead)
        side_own = lambda c: copy(base + 1, c, buf_out, buf_side, partner)
        side_in = lambda c: copy(base + 1, c, buf_in, buf_side, partner)
        passes_in = jnp.logical_and(jnp.logical_not(passes_own), has_in)
        side_arrives = jnp.logical_or(jnp.logical_not(passes_own), has_in)

        def step(c):
            @pl.when(jnp.logical_and(has_in, c == 0))
            def _():
                arrival.wait_recv()

            @pl.when(has_in)
            def _():
                chain(c).wait_recv()

                @pl.when(jnp.logical_not(passes_own))
                def _():
                    side_in(c).start()

                for e in range(2):
                    h = 2 * c + e
                    rows = pl.ds(pl.multiple_of(h * HEAD_DIM, HEAD_DIM), HEAD_DIM)
                    product = d_ref[h] * near[h]
                    buf_out[rows, :] = (source[rows, :] + product * buf_in[rows, :].astype(F32)).astype(BF16)

            @pl.when(jnp.logical_not(has_in))
            def _():
                rows = pl.ds(pl.multiple_of(c * width, width), width)
                buf_out[rows, :] = source[rows, :].astype(BF16)

            @pl.when(passes_own)
            def _():
                side_own(c).start()

            @pl.when(has_next)
            def _():
                chain(c).start()

        def finish(c):
            @pl.when(side_arrives)
            def _():
                side_own(c).wait_recv()

            for e in range(2):
                h = 2 * c + e
                rows = slice(h * HEAD_DIM, (h + 1) * HEAD_DIM)

                @pl.when(has_in)
                def _():
                    source[rows, :] = (
                        buf_side[rows, :].astype(F32) + near[h] * buf_in[rows, :].astype(F32)
                    )

                @pl.when(jnp.logical_and(jnp.logical_not(has_in), side_arrives))
                def _():
                    source[rows, :] = buf_side[rows, :].astype(F32)

                @pl.when(jnp.logical_not(side_arrives))
                def _():
                    source[rows, :] = jnp.zeros((HEAD_DIM, STATE), F32)

        def drain():
            @pl.when(has_next)
            def _():
                settle(buf_out, send_sems.at[base])

            @pl.when(jnp.logical_or(passes_own, passes_in))
            def _():
                settle(buf_out, send_sems.at[base + 1])

        return step, finish, drain

    forward, forward_end, forward_drain = stream(
        0, m > 0, m < columns - 1, k + 2, f_ref, c_in, c_out, c_side, d_prev, to_next, r == 0
    )
    backward, backward_end, backward_drain = stream(
        2, m < columns - 1, m > 0, k - 2, g_ref, b_in, b_out, b_side, d_next, to_prev, r == 1
    )
    lead = LAG * (columns - 1 - 2 * m)
    forward_at = jnp.maximum(-lead, 0)
    backward_at = jnp.maximum(lead, 0)

    def carried(pair):
        group = pair // pairs
        cols = slice(pair * width, (pair + 1) * width)
        cols_g = slice(group * STATE, (group + 1) * STATE)
        forward_end(pair)
        backward_end(pair)
        arrived, ended = f_ref[cols], g_ref[cols]
        starts = [arrived.astype(BF16), (f0_ref[cols] + by_head(0, pair) * arrived).astype(BF16)]
        ends = [(g1_ref[cols] + by_head(1, pair) * ended).astype(BF16), ended.astype(BF16)]
        for number in (0, 1):
            tokens = spans(number)
            grad_x = gx_local[tokens, cols] + spread(2, number, pair) * dot(
                b_ref[tokens, cols_g], ends[number], 1, 1
            )
            gx_ref[tokens, cols] = grad_x.astype(BF16)
            gb_ref[tokens, cols_g] += dot(xw_ref[tokens, cols], ends[number], 1, 0)
            gc_ref[tokens, cols_g] += dot(dyw_ref[tokens, cols], starts[number], 1, 0)
        if pair == group * pairs + pairs - 1:
            for half in (0, 1):
                at = (half * groups + group) * STATE
                gbc_ref[:, at : at + STATE] = (gc_ref if half else gb_ref)[:, cols_g].astype(BF16)
                if whole:
                    gbc_copy(1, group, half).start()
                    gbc_copy(0, group, half).start()

    per_load = max(chunks // 4, 1)
    span_of_steps = LAG * (columns - 1)

    def exchange(s):
        f = s - forward_at
        b = s - backward_at

        @pl.when(jnp.logical_and(f >= 0, f < chunks))
        def _():
            forward(f)

        @pl.when(jnp.logical_and(b >= 0, b < chunks))
        def _():
            backward(b)

    for s in range(chunks + span_of_steps + WAIT):
        if s < chunks:
            if s % per_load == 0:
                loads[3 + 2 * (s // per_load)].wait()
                loads[4 + 2 * (s // per_load)].wait()
            summarize(s)
        if s < chunks + span_of_steps:
            exchange(s)
        if s < chunks:
            local(s)
        if s >= span_of_steps + WAIT:
            carried(s - span_of_steps - WAIT)

    def relay_group(group):
        settle(gbc_in.at[1, :, pl.ds(0, 2 * STATE)], gbc_sems.at[3 + group])
        for half in (0, 1):
            gbc_copy(2, group, half).start()

    settle(w_own, w_sems.at[0])
    settle(w_far, w_sems.at[1])

    if whole:
        settle(w_cross.at[:, 0], cross_sems.at[1])
        for source in (0, 1):
            for axis in (0, 1):
                relay_weights(axis, source).start()
        for group in range(groups - 1):
            relay_group(group)

    def pair_copy(offset, c):
        slot = offset * summed + c
        return pltpu.make_async_remote_copy(
            src_ref=pair_out.at[slot], dst_ref=pair_in.at[slot],
            send_sem=pair_send.at[0], recv_sem=pair_recv.at[slot],
            device_id={"seq": k, "tp": mate}, device_id_type=MESH,
        )

    def chip_copy(offset, c):
        slot = (offset - 1) * summed + c
        return pltpu.make_async_remote_copy(
            src_ref=chip_out.at[slot], dst_ref=chip_in.at[slot],
            send_sem=chip_send.at[0], recv_sem=chip_recv.at[slot],
            device_id={"seq": k, "tp": owner_of(offset, True)}, device_id_type=MESH,
        )

    def partial(offset, same_core, c):
        weights = w_own[c] if offset == 0 and same_core else w_far[far_slot(offset, same_core, c)]
        return dot(gbc_ref[...], weights, 1, 1)

    def give(offset, c):
        pair_out[offset * summed + c] = partial(offset, False, c).astype(BF16)
        pair_copy(offset, c).start()

    def send_on(offset, c):
        own = partial(offset, True, c)
        pair_copy(offset, c).wait_recv()
        slot = offset * summed + c
        chip_out[(offset - 1) * summed + c] = (own + pair_in[slot].astype(F32)).astype(BF16)
        chip_copy(offset, c).start()

    for offset in range(1, chips):
        def body(s, carry):
            @pl.when(s < summed)
            def _():
                give(offset, s)

            @pl.when(s >= 2)
            def _():
                send_on(offset, s - 2)

            return carry

        lax.fori_loop(0, summed + 2, body, 0)

    def near_give(c, carry):
        give(0, c)
        return carry

    lax.fori_loop(0, summed, near_give, 0)

    def gather(g, carry):
        total = dot(gbc_ref[...], w_own[summed + g], 1, 1) + dot(gbc_in[0], w_mate[g], 1, 1)
        total = total + dot(gbc_in[1], w_cross[1, g], 1, 1) + dot(gbc_in[2], w_cross[0, g], 1, 1)
        cols = pl.ds(pl.multiple_of(place(summed + g) * piece, piece), piece)
        out_ref[:, cols] = total.astype(BF16)
        return carry

    if whole:
        relay_group(groups - 1)
        settle(w_mate, mate_sems.at[1])
        settle(w_cross.at[:, 1], cross_sems.at[2])
        settle(gbc_in.at[0], gbc_sems.at[1])
        settle(gbc_in.at[2], gbc_sems.at[2])
        lax.fori_loop(0, 2, gather, 0)

    def final(c, carry):
        total = partial(0, True, c)
        pair_copy(0, c).wait_recv()
        total = total + pair_in[c].astype(F32)
        for offset in range(1, chips):
            chip_copy(offset, c).wait_recv()
            total = total + chip_in[(offset - 1) * summed + c].astype(F32)
        cols = pl.ds(pl.multiple_of(place(c) * piece, piece), piece)
        out_ref[:, cols] = total.astype(BF16)
        return carry

    early = summed - 1 if whole else summed
    lax.fori_loop(0, early, final, 0)
    if whole:
        for axis in (0, 1):
            settle(w_cross.at[:, 2 + axis], relay_sems.at[1 + axis])
        lax.fori_loop(2, whole, gather, 0)
        final(early, 0)

    settle(pair_out, pair_send.at[0])
    settle(chip_out, chip_send.at[0])
    if whole:
        settle(w_cross.at[:, pl.ds(0, 2)], cross_sems.at[0])
        settle(w_mate, mate_sems.at[0])
        settle(w_cross.at[:, pl.ds(0, 2)], relay_sems.at[0])
        settle(gbc_in, gbc_sems.at[0])
    forward_drain()
    backward_drain()

    @pl.when(sends_next)
    def _():
        to_next.wait_send()

    @pl.when(sends_prev)
    def _():
        to_prev.wait_send()


def store_kernel(x_ref, input_ref, x_hbm, input_hbm, sems):
    copies = []
    for i, (held, target) in enumerate(((x_ref, x_hbm), (input_ref, input_hbm))):
        part = held.shape[0] // 4
        for n in range(4):
            rows = pl.ds(n * part, part)
            copies.append(pltpu.make_async_copy(held.at[rows], target.at[rows], sems.at[i, n]))
    for copy in copies:
        copy.start()
    for copy in copies:
        copy.wait()


def per_device(inner_x, in_b, in_c, log_decay, doc_lengths, out_grad, w_b, w_c):
    tokens, inner = inner_x.shape
    heads = log_decay.shape[0]
    seq_count, tp_count = lax.axis_size("seq"), lax.axis_size("tp")
    block = w_b.shape[0] // tp_count
    chips = tp_count // 2
    piece = 256
    pieces = block // piece
    chunks = heads // 2
    wide = in_b.shape[1]
    whole = 4 if chips == 2 and pieces == 8 and seq_count % 4 == 0 else 0
    summed = pieces - whole
    groups = wide // STATE
    vmem = pltpu.VMEM
    dma = pltpu.SemaphoreType.DMA
    row = vmem((heads, 1, STATE), F32)
    square = lambda n: vmem((n, SPAN, SPAN), F32)
    held_x, held_input = pl.pallas_call(
        functools.partial(fused_kernel, seq_count // 2, chips, pieces, whole),
        out_shape=[
            vmem((tokens, inner), BF16),
            vmem((tokens, block), BF16),
        ],
        in_specs=[SMEM] + [ANY] * 7,
        out_specs=[pl.BlockSpec(memory_space=vmem)] * 2,
        scratch_shapes=[
            vmem((tokens, inner), BF16), vmem((tokens, inner), BF16),
            vmem((tokens, wide), BF16), vmem((tokens, wide), BF16),
            vmem((heads, tokens), F32),
            vmem((6, SPAN, heads), F32), vmem((2, heads, SPAN), F32),
            row, row, row,
            square(2), square(2 * groups), square(2 * groups),
            vmem((tokens, inner), BF16), vmem((tokens, inner), BF16),
            vmem((tokens, inner), F32),
            vmem((tokens, wide), F32), vmem((tokens, wide), F32), vmem((tokens, 2 * wide), BF16),
        ]
        + [vmem((inner, STATE), F32)] * 4
        + [vmem((inner, STATE), BF16)] * 6
        + [
            vmem((pieces, piece, 2 * wide), BF16),
            vmem(((2 * chips - 1) * summed, piece, 2 * wide), BF16),
            vmem((chips * summed, tokens, piece), BF16),
            vmem((chips * summed, tokens, piece), BF16),
            vmem(((chips - 1) * summed, tokens, piece), BF16),
            vmem(((chips - 1) * summed, tokens, piece), BF16),
            dma((11,)), dma((2, 2)), dma((4,)), dma((4, chunks)),
            dma((2,)), dma((1,)), dma((chips * summed,)), dma((1,)), dma(((chips - 1) * summed,)),
        ]
        + ([
            vmem((whole, piece, 2 * wide), BF16),
            vmem((2, whole, piece, 2 * wide), BF16),
            vmem((3, tokens, 2 * wide), BF16),
            dma((2,)), dma((3,)), dma((3,)), dma((3 + groups,)),
        ] if whole else []),
        compiler_params=pltpu.CompilerParams(
            collective_id=0, has_side_effects=True, vmem_limit_bytes=56 * 1024 * 1024
        ),
        name="fused",
    )(doc_lengths, inner_x, out_grad, in_b, in_c, log_decay, w_b, w_c)
    return tuple(pl.pallas_call(
        store_kernel,
        out_shape=[
            jax.ShapeDtypeStruct((tokens, inner), BF16),
            jax.ShapeDtypeStruct((tokens, block), BF16),
        ],
        in_specs=[pl.BlockSpec(memory_space=vmem)] * 2,
        out_specs=[ANY] * 2,
        scratch_shapes=[dma((2, 4))],
        name="store",
    )(pltpu.with_memory_space_constraint(held_x, pltpu.VMEM), pltpu.with_memory_space_constraint(held_input, pltpu.VMEM)))


def solution(mesh):
    placed = (
        P("seq", "tp"),
        P("seq", "tp"),
        P("seq", "tp"),
        P("tp", "seq"),
        P(),
        P("seq", "tp"),
        P(None, "tp"),
        P(None, "tp"),
    )
    return jax.shard_map(
        per_device,
        mesh=mesh,
        in_specs=placed,
        out_specs=(P("seq", "tp"), P("seq", "tp")),
        check_vma=False,
    )
```

```python
import functools

import jax
import jax.numpy as jnp
from jax import lax
from jax.experimental import pallas as pl
from jax.experimental.pallas import tpu as pltpu
from jax.sharding import PartitionSpec as P

HEAD_DIM = 64
STATE = 128
SPAN = 128
FIRST = 8
SLOT = 2
HOP = 3
WAIT = 8
EDGE_RELAY = 30
LATER = 6
INNER_RELAY = 40
F32 = jnp.float32
BF16 = jnp.bfloat16
MESH = pl.DeviceIdType.MESH
SMEM = pl.BlockSpec(memory_space=pltpu.SMEM)
ANY = pl.BlockSpec(memory_space=pl.ANY)


def dot(a, b, a_dim, b_dim):
    return lax.dot_general(a, b, (((a_dim,), (b_dim,)), ((), ())), preferred_element_type=F32)


def doc_of(lens_ref, position):
    end = 0
    doc = jnp.zeros_like(position)
    for k in range(lens_ref.shape[0] - 1):
        end = end + lens_ref[k]
        doc = doc + (position >= end).astype(jnp.int32)
    return doc


def span_decays(lens_ref, log_ref, number):
    heads, tokens = log_ref.shape
    first = lax.axis_index("seq") * tokens + number * SPAN
    cumulative = log_ref[:, number * SPAN : (number + 1) * SPAN]
    lane = lax.broadcasted_iota(jnp.int32, (heads, SPAN), 1)
    shift = 1
    while shift < SPAN:
        rolled = pltpu.roll(cumulative, shift, 1)
        cumulative = cumulative + jnp.where(lane >= shift, rolled, 0.0)
        shift *= 2
    doc_row = doc_of(lens_ref, first + lane)
    doc_last = doc_of(lens_ref, jnp.full((heads, SPAN), first + SPAN - 1, jnp.int32))
    before = jnp.full((heads, SPAN), first - 1, jnp.int32)
    doc_prior = jnp.where(before >= 0, doc_of(lens_ref, before), -1)
    last = jnp.broadcast_to(cumulative[:, SPAN - 1 :], (heads, SPAN))
    enter = jnp.where(doc_row == doc_prior, jnp.exp(cumulative), 0.0)
    leave = jnp.where(doc_row == doc_last, jnp.exp(last - cumulative), 0.0)
    total = jnp.where(doc_last == doc_prior, jnp.exp(last), 0.0)
    return cumulative, enter, leave, total


def fused_kernel(
    columns, chips, pieces, whole, lens_ref, x_hbm, dy_hbm, b_hbm, c_hbm, log_hbm, wb_ref, wc_ref, gx_ref, out_ref,
    x_ref, dy_ref, b_ref, c_ref, log_ref, turned, totals, d_ref, d_near, bias, scores, mixed,
    xw_ref, dyw_ref, gx_local, gb_ref, gc_ref, gbc_ref, f0_ref, f_ref, g1_ref, g_ref,
    chain_in, chain_out, own_out, near_in, mid_out, start_in,
    w_own, w_far, pair_out, pair_in, chip_out, chip_in,
    load_sems, d_sems, send_sems, recv_sems,
    w_sems, pair_send, pair_recv, chip_send, chip_recv,
    *shared,
):
    summed = pieces - whole
    if whole:
        w_mate, w_cross, gbc_in, mate_sems, cross_sems, relay_sems, gbc_sems = shared
    heads = log_ref.shape[0]
    groups = b_ref.shape[1] // STATE
    chunks = heads // 2
    pairs = chunks // groups
    width = 2 * HEAD_DIM
    k = lax.axis_index("seq")
    m = k // 2
    r = k - 2 * m
    devices = 2 * columns
    partner = k + 1 - 2 * r
    t = lax.axis_index("tp")
    chip = t // 2
    core = t - 2 * chip
    mate = t + 1 - 2 * core
    block = out_ref.shape[1]
    piece = block // pieces
    depth = wb_ref.shape[1]
    z_at = m - 2 * (m // 2)
    z_mate = k + 2 - 4 * z_at
    here = 2 * z_at + r
    over_y = 2 * z_at + 1 - r
    over_z = 2 * (1 - z_at) + r
    across = 2 * (1 - z_at) + 1 - r

    def place(c):
        if not whole:
            return c
        at = 2 * across
        for first, value in (
            (1, 3 - 2 * r), (2, 5), (3, 7), (4, 2 * here), (5, 2 * r + 1), (6, 2 * over_z), (7, 2 * over_y)
        ):
            at = jnp.where(c >= first, value, at)
        return at

    quarter = x_ref.shape[1] // 4
    loads = [
        pltpu.make_async_copy(log_hbm, log_ref, load_sems.at[0]),
        pltpu.make_async_copy(b_hbm, b_ref, load_sems.at[1]),
        pltpu.make_async_copy(c_hbm, c_ref, load_sems.at[2]),
    ]
    for q in range(4):
        cols = pl.ds(q * quarter, quarter)
        loads.append(pltpu.make_async_copy(x_hbm.at[:, cols], x_ref.at[:, cols], load_sems.at[3 + 2 * q]))
        loads.append(pltpu.make_async_copy(dy_hbm.at[:, cols], dy_ref.at[:, cols], load_sems.at[4 + 2 * q]))
    for load in loads:
        load.start()

    barrier = pltpu.get_barrier_semaphore()
    pl.semaphore_signal(barrier, inc=1, device_id={"seq": partner, "tp": t}, device_id_type=MESH)
    for offset in (-2, 2):
        @pl.when(jnp.logical_and(k + offset >= 0, k + offset < devices))
        def _():
            pl.semaphore_signal(
                barrier, inc=1, device_id={"seq": k + offset, "tp": t}, device_id_type=MESH
            )

    def owner_of(offset, same_core):
        at = lax.rem(chip + offset, chips)
        return 2 * at + (core if same_core else 1 - core)

    pl.semaphore_signal(barrier, inc=1, device_id={"seq": k, "tp": mate}, device_id_type=MESH)
    for offset in range(1, chips):
        pl.semaphore_signal(
            barrier, inc=1, device_id={"seq": k, "tp": owner_of(offset, True)}, device_id_type=MESH
        )
    if whole:
        pl.semaphore_signal(
            barrier, inc=1, device_id={"seq": k, "tp": owner_of(1, False)}, device_id_type=MESH
        )


    def rows_of(offset, same_core, c):
        at = owner_of(offset, same_core) * block + place(c) * piece
        return pl.ds(pl.multiple_of(at, piece), piece)

    def halves(which):
        return pl.ds(which * depth, depth)

    def far_slot(offset, same_core, c):
        return (2 * offset - (1 if offset else 0) + (1 if same_core else 0)) * summed + c

    def w_copy(offset, same_core, c, which):
        own = offset == 0 and same_core
        slot = c if own else far_slot(offset, same_core, c)
        return pltpu.make_async_copy(
            (wb_ref, wc_ref)[which].at[rows_of(offset, same_core, c)],
            (w_own if own else w_far).at[slot, :, halves(which)],
            w_sems.at[0 if own else 1],
        )

    def mate_weights(g, which):
        return pltpu.make_async_remote_copy(
            src_ref=(wb_ref, wc_ref)[which].at[rows_of(0, False, summed + g)],
            dst_ref=w_mate.at[g, :, halves(which)],
            send_sem=mate_sems.at[0], recv_sem=mate_sems.at[1],
            device_id={"seq": k, "tp": mate}, device_id_type=MESH,
        )

    def cross_weights(g, source, which):
        target = 2 * (1 - chip) + source * core + (1 - source) * (1 - core)
        at = pl.multiple_of(target * block + place(summed + g) * piece, piece)
        return pltpu.make_async_remote_copy(
            src_ref=(wb_ref, wc_ref)[which].at[pl.ds(at, piece)],
            dst_ref=w_cross.at[source, g, :, halves(which)],
            send_sem=cross_sems.at[0], recv_sem=cross_sems.at[1 + g],
            device_id={"seq": k, "tp": target}, device_id_type=MESH,
        )

    def relay_weights(source, g):
        return pltpu.make_async_remote_copy(
            src_ref=w_cross.at[source, 1 if g == 1 else 0], dst_ref=w_cross.at[source, g],
            send_sem=relay_sems.at[0], recv_sem=relay_sems.at[1 + source if g == 3 else 2 + g],
            device_id={"seq": partner if g == 3 else z_mate, "tp": t}, device_id_type=MESH,
        )

    def group_columns(group, half):
        return pl.ds(half * groups * STATE + group * STATE, STATE)

    def gbc_copy(kind, group, half):
        cols = group_columns(group, half)
        source = gbc_in.at[1] if kind == 2 else gbc_ref
        return pltpu.make_async_remote_copy(
            src_ref=source.at[:, cols], dst_ref=gbc_in.at[kind, :, cols],
            send_sem=gbc_sems.at[0], recv_sem=gbc_sems.at[3 + group if kind == 1 else 1 + kind // 2],
            device_id={"seq": k, "tp": owner_of(1, True) if kind == 1 else mate}, device_id_type=MESH,
        )

    loads[0].wait()
    low = lax.broadcasted_iota(jnp.int32, (SPAN, width), 1) < HEAD_DIM
    low_mask = low.astype(F32).astype(BF16)
    high_mask = (1.0 - low.astype(F32)).astype(BF16)
    row_id = lax.broadcasted_iota(jnp.int32, (SPAN, SPAN), 0)
    col_id = lax.broadcasted_iota(jnp.int32, (SPAN, SPAN), 1)
    for number in range(2):
        cumulative, enter, leave, total = span_decays(lens_ref, log_ref, number)
        log_ref[:, number * SPAN : (number + 1) * SPAN] = cumulative
        turned[3 * number] = jnp.transpose(cumulative)
        turned[3 * number + 1] = jnp.transpose(enter)
        turned[3 * number + 2] = jnp.transpose(leave)
        totals[number] = total
        first = k * log_ref.shape[1] + number * SPAN
        same = jnp.logical_and(
            doc_of(lens_ref, first + row_id) == doc_of(lens_ref, first + col_id), row_id >= col_id
        )
        bias[number] = jnp.where(same, 0.0, -1e30)
    both = totals[0] * totals[1]
    for h in range(heads):
        d_ref[h] = both[h : h + 1, :]

    count = 1 + jnp.minimum(m, 1) + jnp.minimum(columns - 1 - m, 1) + chips + (1 if whole else 0)
    pl.semaphore_wait(barrier, count)

    def copy(kind, way, j, source, target, to):
        rows = pl.ds(pl.multiple_of(j * width, width), width)
        return pltpu.make_async_remote_copy(
            src_ref=source.at[way, rows], dst_ref=target.at[way, rows],
            send_sem=send_sems.at[kind, way], recv_sem=recv_sems.at[kind, way, j],
            device_id={"seq": to, "tp": t}, device_id_type=MESH,
        )

    def settle(held, sem):
        pltpu.make_async_copy(held, held, sem).wait()

    decays = pltpu.make_async_remote_copy(
        src_ref=d_ref, dst_ref=d_near, send_sem=d_sems.at[0], recv_sem=d_sems.at[1],
        device_id={"seq": partner, "tp": t}, device_id_type=MESH,
    )
    decays.start()

    if whole:
        for which in (0, 1):
            for source in (0, 1):
                cross_weights(0, source, which).start()
        for which in (0, 1):
            cross_weights(1, z_at, which).start()
        for g in range(whole):
            for which in (0, 1):
                mate_weights(g, which).start()

    loads[1].wait()
    loads[2].wait()

    def fetch_weights():
        for offset in range(chips):
            for same_core in (False, True):
                def fetch(c, carry):
                    for which in (0, 1):
                        w_copy(offset, same_core, c, which).start()
                    return carry

                lax.fori_loop(0, pieces if offset == 0 and same_core else summed, fetch, 0)

    def spans(number):
        return slice(number * SPAN, (number + 1) * SPAN)

    def spread(kind, number, pair):
        held = turned.at[3 * number + kind]
        one = jnp.broadcast_to(held[:, 2 * pair : 2 * pair + 1], (SPAN, width))
        two = jnp.broadcast_to(held[:, 2 * pair + 1 : 2 * pair + 2], (SPAN, width))
        return jnp.where(low, one, two)

    def by_head(number, pair):
        return jnp.concatenate(
            [
                jnp.broadcast_to(totals[number, h : h + 1, :], (HEAD_DIM, STATE))
                for h in (2 * pair, 2 * pair + 1)
            ],
            axis=0,
        )

    def summarize(pair):
        group = pair // pairs
        cols = slice(pair * width, (pair + 1) * width)
        cols_g = slice(group * STATE, (group + 1) * STATE)
        states, grads = [], []
        for number in (0, 1):
            tokens = spans(number)
            x_weighted = (x_ref[tokens, cols].astype(F32) * spread(2, number, pair)).astype(BF16)
            dy_weighted = (dy_ref[tokens, cols].astype(F32) * spread(1, number, pair)).astype(BF16)
            xw_ref[tokens, cols] = x_weighted
            dyw_ref[tokens, cols] = dy_weighted
            states.append(dot(x_weighted, b_ref[tokens, cols_g], 0, 0))
            grads.append(dot(dy_weighted, c_ref[tokens, cols_g], 0, 0))
        f0_ref[cols] = states[0]
        f_ref[cols] = states[1] + by_head(1, pair) * states[0]
        g1_ref[cols] = grads[1]
        g_ref[cols] = grads[0] + by_head(0, pair) * grads[1]

    def local(pair):
        group = pair // pairs
        cols = slice(pair * width, (pair + 1) * width)
        cols_g = slice(group * STATE, (group + 1) * STATE)
        for number in (0, 1):
            tokens = spans(number)
            slot = 2 * group + number
            if pair == group * pairs:
                scores[slot] = dot(c_ref[tokens, cols_g], b_ref[tokens, cols_g], 1, 1)
            x_part, dy_part = x_ref[tokens, cols], dy_ref[tokens, cols]
            x_blocks = jnp.concatenate([x_part * low_mask, x_part * high_mask], axis=0)
            dy_blocks = jnp.concatenate([dy_part * low_mask, dy_part * high_mask], axis=0)
            dots = dot(dy_part, x_blocks, 1, 1)
            score_low = []
            added = None
            for e in range(2):
                h = 2 * pair + e
                column = jnp.broadcast_to(turned[3 * number, :, h : h + 1], (SPAN, SPAN))
                gap = column - log_ref[h : h + 1, number * SPAN : (number + 1) * SPAN]
                within = jnp.exp(gap + bias[number])
                term = within * dots[:, e * SPAN : (e + 1) * SPAN]
                added = term if added is None else added + term
                score_low.append((within * scores[slot]).astype(BF16))
            mixed[slot] = added if pair == group * pairs else mixed[slot] + added
            gx_local[tokens, cols] = dot(jnp.concatenate(score_low, axis=0), dy_blocks, 0, 0)
            if pair == group * pairs + pairs - 1:
                mixed_low = mixed[slot].astype(BF16)
                gb_ref[tokens, cols_g] = dot(mixed_low, c_ref[tokens, cols_g], 0, 0)
                gc_ref[tokens, cols_g] = dot(mixed_low, b_ref[tokens, cols_g], 1, 0)

    def stream(way, source):
        first = r == way
        second = jnp.logical_not(first)
        has_in = (m < columns - 1) if way else (m > 0)
        has_next = (m > 0) if way else (m < columns - 1)
        gives = jnp.logical_or(first, has_next)
        own = lambda j: copy(0, way, j, own_out, near_in, partner)
        chain = lambda j: copy(1, way, j, chain_out, chain_in, k - 2 if way else k + 2)
        middle = lambda j: copy(2, way, j, mid_out, start_in, partner)
        passed = lambda j: copy(2, way, j, chain_in, start_in, partner)

        @pl.when(jnp.logical_not(has_in))
        def _():
            chain_in[way] = jnp.zeros(chain_in.shape[1:], BF16)

        def part(j, e):
            rows = pl.ds(pl.multiple_of(j * width + e * HEAD_DIM, HEAD_DIM), HEAD_DIM)
            held = pl.ds(pl.multiple_of((2 * j + r) * width + e * HEAD_DIM, HEAD_DIM), HEAD_DIM)
            return rows, held, 2 * (2 * j + r) + e

        def give(j):
            @pl.when(gives)
            def _():
                away = pl.ds(pl.multiple_of((2 * j + 1 - r) * width, width), width)
                own_out[way, j * width : (j + 1) * width] = source[away, :].astype(BF16)
                own(j).start()

        def step(j):
            @pl.when(has_in)
            def _():
                chain(j).wait_recv()

            @pl.when(first)
            def _():
                for e in range(2):
                    rows, held, h = part(j, e)
                    mid_out[way, rows] = (
                        source[held, :] + d_ref[h] * chain_in[way, rows].astype(F32)
                    ).astype(BF16)
                middle(j).start()

                @pl.when(has_next)
                def _():
                    own(j).wait_recv()
                    for e in range(2):
                        rows, held, h = part(j, e)
                        mid = source[held, :] + d_ref[h] * chain_in[way, rows].astype(F32)
                        chain_out[way, rows] = (
                            near_in[way, rows].astype(F32) + d_near[h] * mid
                        ).astype(BF16)
                    chain(j).start()

                for e in range(2):
                    rows, held, h = part(j, e)
                    source[held, :] = chain_in[way, rows].astype(F32)

            @pl.when(second)
            def _():
                @pl.when(has_in)
                def _():
                    passed(j).start()

                own(j).wait_recv()

                @pl.when(has_next)
                def _():
                    for e in range(2):
                        rows, held, h = part(j, e)
                        mid = near_in[way, rows].astype(F32) + d_near[h] * chain_in[way, rows].astype(F32)
                        chain_out[way, rows] = (source[held, :] + d_ref[h] * mid).astype(BF16)
                    chain(j).start()

                for e in range(2):
                    rows, held, h = part(j, e)
                    source[held, :] = (
                        near_in[way, rows].astype(F32) + d_near[h] * chain_in[way, rows].astype(F32)
                    )

        def finish(c):
            j = c // 2
            rows = slice(c * width, (c + 1) * width)
            away = r == 1 - c % 2
            arrives = jnp.logical_or(second, has_in)

            @pl.when(jnp.logical_and(away, arrives))
            def _():
                middle(j).wait_recv()
                source[rows, :] = start_in[way, j * width : (j + 1) * width].astype(F32)

            @pl.when(jnp.logical_and(away, jnp.logical_not(arrives)))
            def _():
                source[rows, :] = jnp.zeros((width, STATE), F32)

        def drain():
            @pl.when(gives)
            def _():
                settle(own_out.at[way], send_sems.at[0, way])

            @pl.when(has_next)
            def _():
                settle(chain_out.at[way], send_sems.at[1, way])

            @pl.when(jnp.logical_or(first, has_in))
            def _():
                settle(mid_out.at[way], send_sems.at[2, way])

        return give, step, finish, drain

    forward_give, forward, forward_end, forward_drain = stream(0, f_ref)
    backward_give, backward, backward_end, backward_drain = stream(1, g_ref)

    def carried(pair):
        group = pair // pairs
        cols = slice(pair * width, (pair + 1) * width)
        cols_g = slice(group * STATE, (group + 1) * STATE)
        forward_end(pair)
        backward_end(pair)
        arrived, ended = f_ref[cols], g_ref[cols]
        starts = [arrived.astype(BF16), (f0_ref[cols] + by_head(0, pair) * arrived).astype(BF16)]
        ends = [(g1_ref[cols] + by_head(1, pair) * ended).astype(BF16), ended.astype(BF16)]
        for number in (0, 1):
            tokens = spans(number)
            grad_x = gx_local[tokens, cols] + spread(2, number, pair) * dot(
                b_ref[tokens, cols_g], ends[number], 1, 1
            )
            gx_ref[tokens, cols] = grad_x.astype(BF16)
            gb_ref[tokens, cols_g] += dot(xw_ref[tokens, cols], ends[number], 1, 0)
            gc_ref[tokens, cols_g] += dot(dyw_ref[tokens, cols], starts[number], 1, 0)
        if pair == group * pairs + pairs - 1:
            for half in (0, 1):
                at = (half * groups + group) * STATE
                gbc_ref[:, at : at + STATE] = (gc_ref if half else gb_ref)[:, cols_g].astype(BF16)
                if whole:
                    gbc_copy(1, group, half).start()
                    gbc_copy(0, group, half).start()

    per_load = max(chunks // 4, 1)
    rounds = chunks // 2
    last = HOP * (columns - 1)

    def exchange(e):
        f = e - HOP * m
        b = e - HOP * (columns - 1 - m)

        @pl.when(jnp.logical_and(f >= 0, f < rounds))
        def _():
            forward(f)

        @pl.when(jnp.logical_and(b >= 0, b < rounds))
        def _():
            backward(b)

    early = 2 * m < columns

    def give(j, soon):
        @pl.when(early if soon else jnp.logical_not(early))
        def _():
            forward_give(j)

        @pl.when(jnp.logical_not(early) if soon else early)
        def _():
            backward_give(j)

    edge = jnp.logical_or(m == 0, m == columns - 1)
    done = 0
    for s in range(FIRST + SLOT * (last + rounds) + WAIT):
        if s == min(3, chunks - 1):
            fetch_weights()
        if s < chunks:
            if s % per_load == 0:
                loads[3 + 2 * (s // per_load)].wait()
                loads[4 + 2 * (s // per_load)].wait()
            summarize(s)
            if s % 2:
                give(s // 2, True)
        behind = s - LATER
        if behind >= 0 and behind % 2 == 1 and behind < chunks:
            give(behind // 2, False)
        e = (s - FIRST) // SLOT
        if s >= FIRST and (s - FIRST) % SLOT == 0 and e < last + rounds:
            if e == 0:
                decays.wait_recv()
            exchange(e)
        if chunks <= s < 2 * chunks:
            local(s - chunks)
        if whole and s == EDGE_RELAY:
            settle(w_cross.at[:, 0], cross_sems.at[1])
        for at, sends in ((EDGE_RELAY, edge), (INNER_RELAY, jnp.logical_not(edge))):
            if whole and s == at:
                @pl.when(sends)
                def _():
                    for source in (0, 1):
                        relay_weights(source, 2).start()
        if whole and s == INNER_RELAY:
            settle(w_cross.at[0, 1], cross_sems.at[2])
            relay_weights(z_at, 1).start()
        ready = s - FIRST - SLOT * last - WAIT
        if s >= 2 * chunks - 1 and ready >= 0:
            while done < chunks and done < 2 * (ready // SLOT + 1):
                carried(done)
                done += 1
    while done < chunks:
        carried(done)
        done += 1


    def relay_group(group):
        settle(gbc_in.at[1, :, pl.ds(0, 2 * STATE)], gbc_sems.at[3 + group])
        for half in (0, 1):
            gbc_copy(2, group, half).start()

    settle(w_own, w_sems.at[0])
    settle(w_far, w_sems.at[1])

    if whole:
        for source in (0, 1):
            relay_weights(source, 3).start()

    def pair_copy(offset, c):
        slot = offset * summed + c
        return pltpu.make_async_remote_copy(
            src_ref=pair_out.at[slot], dst_ref=pair_in.at[slot],
            send_sem=pair_send.at[0], recv_sem=pair_recv.at[slot],
            device_id={"seq": k, "tp": mate}, device_id_type=MESH,
        )

    def chip_copy(offset, c):
        slot = (offset - 1) * summed + c
        return pltpu.make_async_remote_copy(
            src_ref=chip_out.at[slot], dst_ref=chip_in.at[slot],
            send_sem=chip_send.at[0], recv_sem=chip_recv.at[slot],
            device_id={"seq": k, "tp": owner_of(offset, True)}, device_id_type=MESH,
        )

    def partial(offset, same_core, c):
        weights = w_own[c] if offset == 0 and same_core else w_far[far_slot(offset, same_core, c)]
        return dot(gbc_ref[...], weights, 1, 1)

    def give(offset, c):
        pair_out[offset * summed + c] = partial(offset, False, c).astype(BF16)
        pair_copy(offset, c).start()

    def send_on(offset, c):
        own = partial(offset, True, c)
        pair_copy(offset, c).wait_recv()
        slot = offset * summed + c
        chip_out[(offset - 1) * summed + c] = (own + pair_in[slot].astype(F32)).astype(BF16)
        chip_copy(offset, c).start()

    for offset in range(1, chips):
        def body(s, carry):
            @pl.when(s < summed)
            def _():
                give(offset, s)

            @pl.when(s >= 2)
            def _():
                send_on(offset, s - 2)

            return carry

        lax.fori_loop(0, summed + 2, body, 0)

    def near_give(c, carry):
        give(0, c)
        return carry

    lax.fori_loop(0, summed, near_give, 0)

    def gather(g, carry):
        total = dot(gbc_ref[...], w_own[summed + g], 1, 1) + dot(gbc_in[0], w_mate[g], 1, 1)
        for source, held in ((0, gbc_in.at[2]), (1, gbc_in.at[1])):
            if not isinstance(g, jax.Array) and g == 3:
                settle(w_cross.at[source, 3], relay_sems.at[1 + source])
            total = total + dot(held[...], w_cross[source, g], 1, 1)
        cols = pl.ds(pl.multiple_of(place(summed + g) * piece, piece), piece)
        out_ref[:, cols] = total.astype(BF16)
        return carry

    if whole:
        for group in range(groups):
            relay_group(group)
        settle(w_mate, mate_sems.at[1])
        settle(gbc_in.at[0], gbc_sems.at[1])
        settle(gbc_in.at[2], gbc_sems.at[2])
        gather(0, 0)

    def final(c, carry):
        total = partial(0, True, c)
        pair_copy(0, c).wait_recv()
        total = total + pair_in[c].astype(F32)
        for offset in range(1, chips):
            chip_copy(offset, c).wait_recv()
            total = total + chip_in[(offset - 1) * summed + c].astype(F32)
        cols = pl.ds(pl.multiple_of(place(c) * piece, piece), piece)
        out_ref[:, cols] = total.astype(BF16)
        return carry

    lax.fori_loop(0, summed - 2 if whole else summed, final, 0)
    if whole:
        settle(w_cross.at[:, 2], relay_sems.at[4])
        gather(2, 0)
        final(summed - 2, 0)
        gather(3, 0)
        settle(w_cross.at[0, 1], relay_sems.at[3])
        gather(1, 0)
        final(summed - 1, 0)

    settle(pair_out, pair_send.at[0])
    settle(chip_out, chip_send.at[0])
    if whole:
        settle(w_cross.at[0, pl.ds(0, 3)], cross_sems.at[0])
        settle(w_mate, mate_sems.at[0])
        settle(w_own.at[pl.ds(0, 5)], relay_sems.at[0])
        settle(gbc_in, gbc_sems.at[0])
    forward_drain()
    backward_drain()

    decays.wait_send()


def store_kernel(x_ref, input_ref, x_hbm, input_hbm, sems):
    copies = []
    for i, (held, target) in enumerate(((x_ref, x_hbm), (input_ref, input_hbm))):
        part = held.shape[0] // 4
        for n in range(4):
            rows = pl.ds(n * part, part)
            copies.append(pltpu.make_async_copy(held.at[rows], target.at[rows], sems.at[i, n]))
    for copy in copies:
        copy.start()
    for copy in copies:
        copy.wait()


def per_device(inner_x, in_b, in_c, log_decay, doc_lengths, out_grad, w_b, w_c):
    tokens, inner = inner_x.shape
    heads = log_decay.shape[0]
    seq_count, tp_count = lax.axis_size("seq"), lax.axis_size("tp")
    block = w_b.shape[0] // tp_count
    chips = tp_count // 2
    piece = 256
    pieces = block // piece
    chunks = heads // 2
    wide = in_b.shape[1]
    whole = 4 if chips == 2 and pieces == 8 and seq_count % 4 == 0 else 0
    summed = pieces - whole
    groups = wide // STATE
    vmem = pltpu.VMEM
    dma = pltpu.SemaphoreType.DMA
    row = vmem((heads, 1, STATE), F32)
    square = lambda n: vmem((n, SPAN, SPAN), F32)
    held_x, held_input = pl.pallas_call(
        functools.partial(fused_kernel, seq_count // 2, chips, pieces, whole),
        out_shape=[
            vmem((tokens, inner), BF16),
            vmem((tokens, block), BF16),
        ],
        in_specs=[SMEM] + [ANY] * 7,
        out_specs=[pl.BlockSpec(memory_space=vmem)] * 2,
        scratch_shapes=[
            vmem((tokens, inner), BF16), vmem((tokens, inner), BF16),
            vmem((tokens, wide), BF16), vmem((tokens, wide), BF16),
            vmem((heads, tokens), F32),
            vmem((6, SPAN, heads), F32), vmem((2, heads, SPAN), F32),
            row, row,
            square(2), square(2 * groups), square(2 * groups),
            vmem((tokens, inner), BF16), vmem((tokens, inner), BF16),
            vmem((tokens, inner), F32),
            vmem((tokens, wide), F32), vmem((tokens, wide), F32), vmem((tokens, 2 * wide), BF16),
        ]
        + [vmem((inner, STATE), F32)] * 4
        + [vmem((2, inner // 2, STATE), BF16)] * 6
        + [
            vmem((pieces, piece, 2 * wide), BF16),
            vmem(((2 * chips - 1) * summed, piece, 2 * wide), BF16),
            vmem((chips * summed, tokens, piece), BF16),
            vmem((chips * summed, tokens, piece), BF16),
            vmem(((chips - 1) * summed, tokens, piece), BF16),
            vmem(((chips - 1) * summed, tokens, piece), BF16),
            dma((11,)), dma((2,)), dma((3, 2)), dma((3, 2, chunks // 2)),
            dma((2,)), dma((1,)), dma((chips * summed,)), dma((1,)), dma(((chips - 1) * summed,)),
        ]
        + ([
            vmem((whole, piece, 2 * wide), BF16),
            vmem((2, whole, piece, 2 * wide), BF16),
            vmem((3, tokens, 2 * wide), BF16),
            dma((2,)), dma((3,)), dma((5,)), dma((3 + groups,)),
        ] if whole else []),
        compiler_params=pltpu.CompilerParams(
            collective_id=0, has_side_effects=True, vmem_limit_bytes=56 * 1024 * 1024
        ),
        name="fused",
    )(doc_lengths, inner_x, out_grad, in_b, in_c, log_decay, w_b, w_c)
    return tuple(pl.pallas_call(
        store_kernel,
        out_shape=[
            jax.ShapeDtypeStruct((tokens, inner), BF16),
            jax.ShapeDtypeStruct((tokens, block), BF16),
        ],
        in_specs=[pl.BlockSpec(memory_space=vmem)] * 2,
        out_specs=[ANY] * 2,
        scratch_shapes=[dma((2, 4))],
        name="store",
    )(pltpu.with_memory_space_constraint(held_x, pltpu.VMEM), pltpu.with_memory_space_constraint(held_input, pltpu.VMEM)))


def solution(mesh):
    placed = (
        P("seq", "tp"),
        P("seq", "tp"),
        P("seq", "tp"),
        P("tp", "seq"),
        P(),
        P("seq", "tp"),
        P(None, "tp"),
        P(None, "tp"),
    )
    return jax.shard_map(
        per_device,
        mesh=mesh,
        in_specs=placed,
        out_specs=(P("seq", "tp"), P("seq", "tp")),
        check_vma=False,
    )
```

```python
import functools

import jax
import jax.numpy as jnp
from jax import lax
from jax.experimental import pallas as pl
from jax.experimental.pallas import tpu as pltpu
from jax.sharding import PartitionSpec as P

HEAD_DIM = 64
STATE = 128
SPAN = 128
FIRST = 8
SLOT = 2
HOP = 3
WAIT = 8
EDGE_RELAY = 30
LATER = 6
INNER_RELAY = 36
F32 = jnp.float32
BF16 = jnp.bfloat16
MESH = pl.DeviceIdType.MESH
SMEM = pl.BlockSpec(memory_space=pltpu.SMEM)
ANY = pl.BlockSpec(memory_space=pl.ANY)


def dot(a, b, a_dim, b_dim):
    return lax.dot_general(a, b, (((a_dim,), (b_dim,)), ((), ())), preferred_element_type=F32)


def doc_of(lens_ref, position):
    end = 0
    doc = jnp.zeros_like(position)
    for k in range(lens_ref.shape[0] - 1):
        end = end + lens_ref[k]
        doc = doc + (position >= end).astype(jnp.int32)
    return doc


def span_decays(lens_ref, log_ref, number):
    heads, tokens = log_ref.shape
    first = lax.axis_index("seq") * tokens + number * SPAN
    cumulative = log_ref[:, number * SPAN : (number + 1) * SPAN]
    lane = lax.broadcasted_iota(jnp.int32, (heads, SPAN), 1)
    shift = 1
    while shift < SPAN:
        rolled = pltpu.roll(cumulative, shift, 1)
        cumulative = cumulative + jnp.where(lane >= shift, rolled, 0.0)
        shift *= 2
    doc_row = doc_of(lens_ref, first + lane)
    doc_last = doc_of(lens_ref, jnp.full((heads, SPAN), first + SPAN - 1, jnp.int32))
    before = jnp.full((heads, SPAN), first - 1, jnp.int32)
    doc_prior = jnp.where(before >= 0, doc_of(lens_ref, before), -1)
    last = jnp.broadcast_to(cumulative[:, SPAN - 1 :], (heads, SPAN))
    enter = jnp.where(doc_row == doc_prior, jnp.exp(cumulative), 0.0)
    leave = jnp.where(doc_row == doc_last, jnp.exp(last - cumulative), 0.0)
    total = jnp.where(doc_last == doc_prior, jnp.exp(last), 0.0)
    return cumulative, enter, leave, total


def fused_kernel(
    columns, chips, pieces, whole, lens_ref, x_hbm, dy_hbm, b_hbm, c_hbm, log_hbm, wb_ref, wc_ref, gx_ref, out_ref,
    x_ref, dy_ref, b_ref, c_ref, log_ref, turned, totals, d_ref, d_near, bias, scores, mixed,
    xw_ref, dyw_ref, gx_local, gb_ref, gc_ref, gbc_ref, f0_ref, f_ref, g1_ref, g_ref,
    chain_in, chain_out, own_out, near_in, mid_out, start_in,
    w_own, w_far, pair_out, pair_in, chip_out, chip_in,
    load_sems, d_sems, send_sems, recv_sems,
    w_sems, pair_send, pair_recv, chip_send, chip_recv,
    *shared,
):
    summed = pieces - whole
    if whole:
        w_mate, w_cross, gbc_in, mate_sems, cross_sems, relay_sems, gbc_sems = shared[:7]
        mate_part, cross_part, pair_part_out, pair_part_in, chip_part_out, chip_part_in, part_sems = shared[7:]
    lead = summed - 1 if whole else summed
    heads = log_ref.shape[0]
    groups = b_ref.shape[1] // STATE
    chunks = heads // 2
    pairs = chunks // groups
    width = 2 * HEAD_DIM
    k = lax.axis_index("seq")
    m = k // 2
    r = k - 2 * m
    devices = 2 * columns
    partner = k + 1 - 2 * r
    t = lax.axis_index("tp")
    chip = t // 2
    core = t - 2 * chip
    mate = t + 1 - 2 * core
    block = out_ref.shape[1]
    piece = block // pieces
    depth = wb_ref.shape[1]
    z_at = m - 2 * (m // 2)
    z_mate = k + 2 - 4 * z_at
    here = 2 * z_at + r
    over_y = 2 * z_at + 1 - r
    over_z = 2 * (1 - z_at) + r
    across = 2 * (1 - z_at) + 1 - r

    def place(c):
        if not whole:
            return c
        at = 2 * across
        for first, value in (
            (1, 3 - 2 * r), (2, 5), (3, 7), (4, 2 * here), (5, 2 * r + 1), (6, 2 * over_z), (7, 2 * over_y)
        ):
            at = jnp.where(c >= first, value, at)
        return at

    quarter = x_ref.shape[1] // 4
    loads = [
        pltpu.make_async_copy(log_hbm, log_ref, load_sems.at[0]),
        pltpu.make_async_copy(b_hbm, b_ref, load_sems.at[1]),
        pltpu.make_async_copy(c_hbm, c_ref, load_sems.at[2]),
    ]
    for q in range(4):
        cols = pl.ds(q * quarter, quarter)
        loads.append(pltpu.make_async_copy(x_hbm.at[:, cols], x_ref.at[:, cols], load_sems.at[3 + 2 * q]))
        loads.append(pltpu.make_async_copy(dy_hbm.at[:, cols], dy_ref.at[:, cols], load_sems.at[4 + 2 * q]))
    for load in loads:
        load.start()

    barrier = pltpu.get_barrier_semaphore()
    pl.semaphore_signal(barrier, inc=1, device_id={"seq": partner, "tp": t}, device_id_type=MESH)
    for offset in (-2, 2):
        @pl.when(jnp.logical_and(k + offset >= 0, k + offset < devices))
        def _():
            pl.semaphore_signal(
                barrier, inc=1, device_id={"seq": k + offset, "tp": t}, device_id_type=MESH
            )

    def owner_of(offset, same_core):
        at = lax.rem(chip + offset, chips)
        return 2 * at + (core if same_core else 1 - core)

    pl.semaphore_signal(barrier, inc=1, device_id={"seq": k, "tp": mate}, device_id_type=MESH)
    for offset in range(1, chips):
        pl.semaphore_signal(
            barrier, inc=1, device_id={"seq": k, "tp": owner_of(offset, True)}, device_id_type=MESH
        )
    if whole:
        pl.semaphore_signal(
            barrier, inc=1, device_id={"seq": k, "tp": owner_of(1, False)}, device_id_type=MESH
        )


    def rows_of(offset, same_core, c):
        at = owner_of(offset, same_core) * block + place(c) * piece
        return pl.ds(pl.multiple_of(at, piece), piece)

    def halves(which):
        return pl.ds(which * depth, depth)

    def far_slot(offset, same_core, c):
        return (2 * offset - (1 if offset else 0) + (1 if same_core else 0)) * summed + c

    def w_copy(offset, same_core, c, which):
        own = offset == 0 and same_core
        slot = c if own else far_slot(offset, same_core, c)
        return pltpu.make_async_copy(
            (wb_ref, wc_ref)[which].at[rows_of(offset, same_core, c)],
            (w_own if own else w_far).at[slot, :, halves(which)],
            w_sems.at[0 if own else 1],
        )

    def mate_weights(g, which):
        return pltpu.make_async_remote_copy(
            src_ref=(wb_ref, wc_ref)[which].at[rows_of(0, False, summed + g)],
            dst_ref=w_mate.at[g, :, halves(which)],
            send_sem=mate_sems.at[0], recv_sem=mate_sems.at[1],
            device_id={"seq": k, "tp": mate}, device_id_type=MESH,
        )

    def cross_weights(g, source, which):
        target = 2 * (1 - chip) + source * core + (1 - source) * (1 - core)
        at = pl.multiple_of(target * block + place(summed + g) * piece, piece)
        return pltpu.make_async_remote_copy(
            src_ref=(wb_ref, wc_ref)[which].at[pl.ds(at, piece)],
            dst_ref=w_cross.at[source, g, :, halves(which)],
            send_sem=cross_sems.at[0], recv_sem=cross_sems.at[1 + g],
            device_id={"seq": k, "tp": target}, device_id_type=MESH,
        )

    def part_weights(source, which):
        target = mate if source is None else 2 * (1 - chip) + source * core + (1 - source) * (1 - core)
        at = pl.multiple_of(target * block + place(lead) * piece + piece // 2, piece // 2)
        to = mate_part if source is None else cross_part.at[source]
        first = 2 if source is None else 0
        return pltpu.make_async_remote_copy(
            src_ref=(wb_ref, wc_ref)[which].at[pl.ds(at, piece // 2)], dst_ref=to.at[:, halves(which)],
            send_sem=part_sems.at[first], recv_sem=part_sems.at[first + 1],
            device_id={"seq": k, "tp": target}, device_id_type=MESH,
        )

    def relay_weights(source, g):
        return pltpu.make_async_remote_copy(
            src_ref=w_cross.at[source, 1 if g == 1 else 0], dst_ref=w_cross.at[source, g],
            send_sem=relay_sems.at[0], recv_sem=relay_sems.at[1 + source if g == 3 else 2 + g],
            device_id={"seq": partner if g == 3 else z_mate, "tp": t}, device_id_type=MESH,
        )

    def group_columns(group, half):
        return pl.ds(half * groups * STATE + group * STATE, STATE)

    def gbc_copy(kind, group, half):
        cols = group_columns(group, half)
        source = gbc_in.at[1] if kind == 2 else gbc_ref
        return pltpu.make_async_remote_copy(
            src_ref=source.at[:, cols], dst_ref=gbc_in.at[kind, :, cols],
            send_sem=gbc_sems.at[0], recv_sem=gbc_sems.at[3 + group if kind == 1 else 1 + kind // 2],
            device_id={"seq": k, "tp": owner_of(1, True) if kind == 1 else mate}, device_id_type=MESH,
        )

    loads[0].wait()
    low = lax.broadcasted_iota(jnp.int32, (SPAN, width), 1) < HEAD_DIM
    low_mask = low.astype(F32).astype(BF16)
    high_mask = (1.0 - low.astype(F32)).astype(BF16)
    row_id = lax.broadcasted_iota(jnp.int32, (SPAN, SPAN), 0)
    col_id = lax.broadcasted_iota(jnp.int32, (SPAN, SPAN), 1)
    for number in range(2):
        cumulative, enter, leave, total = span_decays(lens_ref, log_ref, number)
        log_ref[:, number * SPAN : (number + 1) * SPAN] = cumulative
        turned[3 * number] = jnp.transpose(cumulative)
        turned[3 * number + 1] = jnp.transpose(enter)
        turned[3 * number + 2] = jnp.transpose(leave)
        totals[number] = total
        first = k * log_ref.shape[1] + number * SPAN
        same = jnp.logical_and(
            doc_of(lens_ref, first + row_id) == doc_of(lens_ref, first + col_id), row_id >= col_id
        )
        bias[number] = jnp.where(same, 0.0, -1e30)
    both = totals[0] * totals[1]
    for h in range(heads):
        d_ref[h] = both[h : h + 1, :]

    count = 1 + jnp.minimum(m, 1) + jnp.minimum(columns - 1 - m, 1) + chips + (1 if whole else 0)
    pl.semaphore_wait(barrier, count)

    def copy(kind, way, j, source, target, to):
        rows = pl.ds(pl.multiple_of(j * width, width), width)
        return pltpu.make_async_remote_copy(
            src_ref=source.at[way, rows], dst_ref=target.at[way, rows],
            send_sem=send_sems.at[kind, way], recv_sem=recv_sems.at[kind, way, j],
            device_id={"seq": to, "tp": t}, device_id_type=MESH,
        )

    def settle(held, sem):
        pltpu.make_async_copy(held, held, sem).wait()

    decays = pltpu.make_async_remote_copy(
        src_ref=d_ref, dst_ref=d_near, send_sem=d_sems.at[0], recv_sem=d_sems.at[1],
        device_id={"seq": partner, "tp": t}, device_id_type=MESH,
    )
    decays.start()

    if whole:
        for which in (0, 1):
            for source in (0, 1):
                cross_weights(0, source, which).start()
        for which in (0, 1):
            cross_weights(1, z_at, which).start()
        for which in (0, 1):
            for source in (0, 1, None):
                part_weights(source, which).start()
        for g in range(whole):
            for which in (0, 1):
                mate_weights(g, which).start()

    loads[1].wait()
    loads[2].wait()

    def fetch_weights():
        for offset in range(chips):
            for same_core in (False, True):
                def fetch(c, carry):
                    for which in (0, 1):
                        w_copy(offset, same_core, c, which).start()
                    return carry

                lax.fori_loop(0, pieces if offset == 0 and same_core else summed, fetch, 0)

    def spans(number):
        return slice(number * SPAN, (number + 1) * SPAN)

    def spread(kind, number, pair):
        held = turned.at[3 * number + kind]
        one = jnp.broadcast_to(held[:, 2 * pair : 2 * pair + 1], (SPAN, width))
        two = jnp.broadcast_to(held[:, 2 * pair + 1 : 2 * pair + 2], (SPAN, width))
        return jnp.where(low, one, two)

    def by_head(number, pair):
        return jnp.concatenate(
            [
                jnp.broadcast_to(totals[number, h : h + 1, :], (HEAD_DIM, STATE))
                for h in (2 * pair, 2 * pair + 1)
            ],
            axis=0,
        )

    def summarize(pair):
        group = pair // pairs
        cols = slice(pair * width, (pair + 1) * width)
        cols_g = slice(group * STATE, (group + 1) * STATE)
        states, grads = [], []
        for number in (0, 1):
            tokens = spans(number)
            x_weighted = (x_ref[tokens, cols].astype(F32) * spread(2, number, pair)).astype(BF16)
            dy_weighted = (dy_ref[tokens, cols].astype(F32) * spread(1, number, pair)).astype(BF16)
            xw_ref[tokens, cols] = x_weighted
            dyw_ref[tokens, cols] = dy_weighted
            states.append(dot(x_weighted, b_ref[tokens, cols_g], 0, 0))
            grads.append(dot(dy_weighted, c_ref[tokens, cols_g], 0, 0))
        f0_ref[cols] = states[0]
        f_ref[cols] = states[1] + by_head(1, pair) * states[0]
        g1_ref[cols] = grads[1]
        g_ref[cols] = grads[0] + by_head(0, pair) * grads[1]

    def local(pair):
        group = pair // pairs
        cols = slice(pair * width, (pair + 1) * width)
        cols_g = slice(group * STATE, (group + 1) * STATE)
        for number in (0, 1):
            tokens = spans(number)
            slot = 2 * group + number
            if pair == group * pairs:
                scores[slot] = dot(c_ref[tokens, cols_g], b_ref[tokens, cols_g], 1, 1)
            x_part, dy_part = x_ref[tokens, cols], dy_ref[tokens, cols]
            x_blocks = jnp.concatenate([x_part * low_mask, x_part * high_mask], axis=0)
            dy_blocks = jnp.concatenate([dy_part * low_mask, dy_part * high_mask], axis=0)
            dots = dot(dy_part, x_blocks, 1, 1)
            score_low = []
            added = None
            for e in range(2):
                h = 2 * pair + e
                column = jnp.broadcast_to(turned[3 * number, :, h : h + 1], (SPAN, SPAN))
                gap = column - log_ref[h : h + 1, number * SPAN : (number + 1) * SPAN]
                within = jnp.exp(gap + bias[number])
                term = within * dots[:, e * SPAN : (e + 1) * SPAN]
                added = term if added is None else added + term
                score_low.append((within * scores[slot]).astype(BF16))
            mixed[slot] = added if pair == group * pairs else mixed[slot] + added
            gx_local[tokens, cols] = dot(jnp.concatenate(score_low, axis=0), dy_blocks, 0, 0)
            if pair == group * pairs + pairs - 1:
                mixed_low = mixed[slot].astype(BF16)
                gb_ref[tokens, cols_g] = dot(mixed_low, c_ref[tokens, cols_g], 0, 0)
                gc_ref[tokens, cols_g] = dot(mixed_low, b_ref[tokens, cols_g], 1, 0)

    def stream(way, source):
        first = r == way
        second = jnp.logical_not(first)
        has_in = (m < columns - 1) if way else (m > 0)
        has_next = (m > 0) if way else (m < columns - 1)
        gives = jnp.logical_or(first, has_next)
        own = lambda j: copy(0, way, j, own_out, near_in, partner)
        chain = lambda j: copy(1, way, j, chain_out, chain_in, k - 2 if way else k + 2)
        middle = lambda j: copy(2, way, j, mid_out, start_in, partner)
        passed = lambda j: copy(2, way, j, chain_in, start_in, partner)

        @pl.when(jnp.logical_not(has_in))
        def _():
            chain_in[way] = jnp.zeros(chain_in.shape[1:], BF16)

        def part(j, e):
            rows = pl.ds(pl.multiple_of(j * width + e * HEAD_DIM, HEAD_DIM), HEAD_DIM)
            held = pl.ds(pl.multiple_of((2 * j + r) * width + e * HEAD_DIM, HEAD_DIM), HEAD_DIM)
            return rows, held, 2 * (2 * j + r) + e

        def give(j):
            @pl.when(gives)
            def _():
                away = pl.ds(pl.multiple_of((2 * j + 1 - r) * width, width), width)
                own_out[way, j * width : (j + 1) * width] = source[away, :].astype(BF16)
                own(j).start()

        def step(j):
            @pl.when(has_in)
            def _():
                chain(j).wait_recv()

            @pl.when(first)
            def _():
                for e in range(2):
                    rows, held, h = part(j, e)
                    mid_out[way, rows] = (
                        source[held, :] + d_ref[h] * chain_in[way, rows].astype(F32)
                    ).astype(BF16)
                middle(j).start()

                @pl.when(has_next)
                def _():
                    own(j).wait_recv()
                    for e in range(2):
                        rows, held, h = part(j, e)
                        mid = source[held, :] + d_ref[h] * chain_in[way, rows].astype(F32)
                        chain_out[way, rows] = (
                            near_in[way, rows].astype(F32) + d_near[h] * mid
                        ).astype(BF16)
                    chain(j).start()

                for e in range(2):
                    rows, held, h = part(j, e)
                    source[held, :] = chain_in[way, rows].astype(F32)

            @pl.when(second)
            def _():
                @pl.when(has_in)
                def _():
                    passed(j).start()

                own(j).wait_recv()

                @pl.when(has_next)
                def _():
                    for e in range(2):
                        rows, held, h = part(j, e)
                        mid = near_in[way, rows].astype(F32) + d_near[h] * chain_in[way, rows].astype(F32)
                        chain_out[way, rows] = (source[held, :] + d_ref[h] * mid).astype(BF16)
                    chain(j).start()

                for e in range(2):
                    rows, held, h = part(j, e)
                    source[held, :] = (
                        near_in[way, rows].astype(F32) + d_near[h] * chain_in[way, rows].astype(F32)
                    )

        def finish(c):
            j = c // 2
            rows = slice(c * width, (c + 1) * width)
            away = r == 1 - c % 2
            arrives = jnp.logical_or(second, has_in)

            @pl.when(jnp.logical_and(away, arrives))
            def _():
                middle(j).wait_recv()
                source[rows, :] = start_in[way, j * width : (j + 1) * width].astype(F32)

            @pl.when(jnp.logical_and(away, jnp.logical_not(arrives)))
            def _():
                source[rows, :] = jnp.zeros((width, STATE), F32)

        def drain():
            @pl.when(gives)
            def _():
                settle(own_out.at[way], send_sems.at[0, way])

            @pl.when(has_next)
            def _():
                settle(chain_out.at[way], send_sems.at[1, way])

            @pl.when(jnp.logical_or(first, has_in))
            def _():
                settle(mid_out.at[way], send_sems.at[2, way])

        return give, step, finish, drain

    forward_give, forward, forward_end, forward_drain = stream(0, f_ref)
    backward_give, backward, backward_end, backward_drain = stream(1, g_ref)

    def carried(pair):
        group = pair // pairs
        cols = slice(pair * width, (pair + 1) * width)
        cols_g = slice(group * STATE, (group + 1) * STATE)
        forward_end(pair)
        backward_end(pair)
        arrived, ended = f_ref[cols], g_ref[cols]
        starts = [arrived.astype(BF16), (f0_ref[cols] + by_head(0, pair) * arrived).astype(BF16)]
        ends = [(g1_ref[cols] + by_head(1, pair) * ended).astype(BF16), ended.astype(BF16)]
        for number in (0, 1):
            tokens = spans(number)
            grad_x = gx_local[tokens, cols] + spread(2, number, pair) * dot(
                b_ref[tokens, cols_g], ends[number], 1, 1
            )
            gx_ref[tokens, cols] = grad_x.astype(BF16)
            gb_ref[tokens, cols_g] += dot(xw_ref[tokens, cols], ends[number], 1, 0)
            gc_ref[tokens, cols_g] += dot(dyw_ref[tokens, cols], starts[number], 1, 0)
        if pair == group * pairs + pairs - 1:
            for half in (0, 1):
                at = (half * groups + group) * STATE
                gbc_ref[:, at : at + STATE] = (gc_ref if half else gb_ref)[:, cols_g].astype(BF16)
                if whole:
                    gbc_copy(1, group, half).start()
                    gbc_copy(0, group, half).start()

    per_load = max(chunks // 4, 1)
    rounds = chunks // 2
    last = HOP * (columns - 1)

    def exchange(e):
        f = e - HOP * m
        b = e - HOP * (columns - 1 - m)

        @pl.when(jnp.logical_and(f >= 0, f < rounds))
        def _():
            forward(f)

        @pl.when(jnp.logical_and(b >= 0, b < rounds))
        def _():
            backward(b)

    early = 2 * m < columns

    def give(j, soon):
        @pl.when(early if soon else jnp.logical_not(early))
        def _():
            forward_give(j)

        @pl.when(jnp.logical_not(early) if soon else early)
        def _():
            backward_give(j)

    edge = jnp.logical_or(m == 0, m == columns - 1)
    done = 0
    for s in range(FIRST + SLOT * (last + rounds) + WAIT):
        if s == min(3, chunks - 1):
            fetch_weights()
        if s < chunks:
            if s % per_load == 0:
                loads[3 + 2 * (s // per_load)].wait()
                loads[4 + 2 * (s // per_load)].wait()
            summarize(s)
            if s % 2:
                give(s // 2, True)
        behind = s - LATER
        if behind >= 0 and behind % 2 == 1 and behind < chunks:
            give(behind // 2, False)
        e = (s - FIRST) // SLOT
        if s >= FIRST and (s - FIRST) % SLOT == 0 and e < last + rounds:
            if e == 0:
                decays.wait_recv()
            exchange(e)
        if chunks <= s < 2 * chunks:
            local(s - chunks)
        if whole and s == EDGE_RELAY:
            settle(w_cross.at[:, 0], cross_sems.at[1])
        for at, sends in ((EDGE_RELAY, edge), (INNER_RELAY, jnp.logical_not(edge))):
            if whole and s == at:
                @pl.when(sends)
                def _():
                    for source in (0, 1):
                        relay_weights(source, 2).start()
        if whole and s == INNER_RELAY:
            settle(w_cross.at[0, 1], cross_sems.at[2])
            relay_weights(z_at, 1).start()
        ready = s - FIRST - SLOT * last - WAIT
        if s >= 2 * chunks - 1 and ready >= 0:
            while done < chunks and done < 2 * (ready // SLOT + 1):
                carried(done)
                done += 1
    while done < chunks:
        carried(done)
        done += 1


    def relay_group(group):
        settle(gbc_in.at[1, :, pl.ds(0, 2 * STATE)], gbc_sems.at[3 + group])
        for half in (0, 1):
            gbc_copy(2, group, half).start()

    settle(w_own, w_sems.at[0])
    settle(w_far, w_sems.at[1])

    if whole:
        for source in (0, 1):
            relay_weights(source, 3).start()

    def pair_copy(offset, c):
        slot = offset * lead + c
        return pltpu.make_async_remote_copy(
            src_ref=pair_out.at[slot], dst_ref=pair_in.at[slot],
            send_sem=pair_send.at[0], recv_sem=pair_recv.at[slot],
            device_id={"seq": k, "tp": mate}, device_id_type=MESH,
        )

    def chip_copy(offset, c):
        slot = (offset - 1) * lead + c
        return pltpu.make_async_remote_copy(
            src_ref=chip_out.at[slot], dst_ref=chip_in.at[slot],
            send_sem=chip_send.at[0], recv_sem=chip_recv.at[slot],
            device_id={"seq": k, "tp": owner_of(offset, True)}, device_id_type=MESH,
        )

    def partial(offset, same_core, c):
        weights = w_own[c] if offset == 0 and same_core else w_far[far_slot(offset, same_core, c)]
        return dot(gbc_ref[...], weights, 1, 1)

    def give(offset, c):
        pair_out[offset * lead + c] = partial(offset, False, c).astype(BF16)
        pair_copy(offset, c).start()

    def send_on(offset, c):
        own = partial(offset, True, c)
        pair_copy(offset, c).wait_recv()
        slot = offset * lead + c
        chip_out[(offset - 1) * lead + c] = (own + pair_in[slot].astype(F32)).astype(BF16)
        chip_copy(offset, c).start()

    def pair_part(offset):
        return pltpu.make_async_remote_copy(
            src_ref=pair_part_out.at[offset], dst_ref=pair_part_in.at[offset],
            send_sem=part_sems.at[4], recv_sem=part_sems.at[5 + offset],
            device_id={"seq": k, "tp": mate}, device_id_type=MESH,
        )

    def chip_part():
        return pltpu.make_async_remote_copy(
            src_ref=chip_part_out, dst_ref=chip_part_in,
            send_sem=part_sems.at[7], recv_sem=part_sems.at[8],
            device_id={"seq": k, "tp": owner_of(1, True)}, device_id_type=MESH,
        )

    low_rows, high_rows = pl.ds(0, piece // 2), pl.ds(piece // 2, piece // 2)

    def give_part(offset):
        weights = w_far[far_slot(offset, False, lead), low_rows]
        pair_part_out[offset] = dot(gbc_ref[...], weights, 1, 1).astype(BF16)
        pair_part(offset).start()

    if whole:
        give_part(1)

    for offset in range(1, chips):
        def body(s, carry):
            @pl.when(s < lead)
            def _():
                give(offset, s)

            @pl.when(s >= 2)
            def _():
                send_on(offset, s - 2)

            return carry

        lax.fori_loop(0, lead + 2, body, 0)

    if whole:
        own = dot(gbc_ref[...], w_far[far_slot(1, True, lead), low_rows], 1, 1)
        pair_part(1).wait_recv()
        chip_part_out[...] = (own + pair_part_in[1].astype(F32)).astype(BF16)
        chip_part().start()

    def near_give(c, carry):
        give(0, c)
        return carry

    lax.fori_loop(0, lead, near_give, 0)
    if whole:
        give_part(0)

    def gather(g, carry):
        total = dot(gbc_ref[...], w_own[summed + g], 1, 1) + dot(gbc_in[0], w_mate[g], 1, 1)
        for source, held in ((0, gbc_in.at[2]), (1, gbc_in.at[1])):
            if not isinstance(g, jax.Array) and g == 3:
                settle(w_cross.at[source, 3], relay_sems.at[1 + source])
            total = total + dot(held[...], w_cross[source, g], 1, 1)
        cols = pl.ds(pl.multiple_of(place(summed + g) * piece, piece), piece)
        out_ref[:, cols] = total.astype(BF16)
        return carry

    if whole:
        for group in range(groups):
            relay_group(group)
        settle(w_mate, mate_sems.at[1])
        settle(gbc_in.at[0], gbc_sems.at[1])
        settle(gbc_in.at[2], gbc_sems.at[2])
        gather(0, 0)
        settle(mate_part, part_sems.at[3])
        settle(cross_part, part_sems.at[1])
        total = dot(gbc_ref[...], w_own[lead, high_rows], 1, 1) + dot(gbc_in[0], mate_part[...], 1, 1)
        total = total + dot(gbc_in[2], cross_part[0], 1, 1) + dot(gbc_in[1], cross_part[1], 1, 1)
        split = place(lead) * piece
        out_ref[:, pl.ds(pl.multiple_of(split + piece // 2, piece // 2), piece // 2)] = total.astype(BF16)

    def final(c, carry):
        total = partial(0, True, c)
        pair_copy(0, c).wait_recv()
        total = total + pair_in[c].astype(F32)
        for offset in range(1, chips):
            chip_copy(offset, c).wait_recv()
            total = total + chip_in[(offset - 1) * lead + c].astype(F32)
        cols = pl.ds(pl.multiple_of(place(c) * piece, piece), piece)
        out_ref[:, cols] = total.astype(BF16)
        return carry

    lax.fori_loop(0, lead - 1 if whole else lead, final, 0)
    if whole:
        settle(w_cross.at[:, 2], relay_sems.at[4])
        gather(2, 0)
        settle(w_cross.at[0, 1], relay_sems.at[3])
        gather(1, 0)
        final(lead - 1, 0)
        gather(3, 0)
        total = dot(gbc_ref[...], w_own[lead, low_rows], 1, 1)
        pair_part(0).wait_recv()
        total = total + pair_part_in[0].astype(F32)
        chip_part().wait_recv()
        total = total + chip_part_in[...].astype(F32)
        out_ref[:, pl.ds(pl.multiple_of(split, piece // 2), piece // 2)] = total.astype(BF16)

    settle(pair_out, pair_send.at[0])
    settle(chip_out, chip_send.at[0])
    if whole:
        settle(w_cross.at[0, pl.ds(0, 3)], cross_sems.at[0])
        settle(w_mate, mate_sems.at[0])
        settle(cross_part, part_sems.at[0])
        settle(mate_part, part_sems.at[2])
        settle(pair_part_out, part_sems.at[4])
        settle(chip_part_out, part_sems.at[7])
        settle(w_own.at[pl.ds(0, 5)], relay_sems.at[0])
        settle(gbc_in, gbc_sems.at[0])
    forward_drain()
    backward_drain()

    decays.wait_send()


def store_kernel(x_ref, input_ref, x_hbm, input_hbm, sems):
    copies = []
    for i, (held, target) in enumerate(((x_ref, x_hbm), (input_ref, input_hbm))):
        part = held.shape[0]
        for n in range(1):
            rows = pl.ds(n * part, part)
            copies.append(pltpu.make_async_copy(held.at[rows], target.at[rows], sems.at[i, n]))
    for copy in copies:
        copy.start()
    for copy in copies:
        copy.wait()


def per_device(inner_x, in_b, in_c, log_decay, doc_lengths, out_grad, w_b, w_c):
    tokens, inner = inner_x.shape
    heads = log_decay.shape[0]
    seq_count, tp_count = lax.axis_size("seq"), lax.axis_size("tp")
    block = w_b.shape[0] // tp_count
    chips = tp_count // 2
    piece = 256
    pieces = block // piece
    chunks = heads // 2
    wide = in_b.shape[1]
    whole = 4 if chips == 2 and pieces == 8 and seq_count % 4 == 0 else 0
    summed = pieces - whole
    lead = summed - 1 if whole else summed
    groups = wide // STATE
    vmem = pltpu.VMEM
    dma = pltpu.SemaphoreType.DMA
    row = vmem((heads, 1, STATE), F32)
    square = lambda n: vmem((n, SPAN, SPAN), F32)
    held_x, held_input = pl.pallas_call(
        functools.partial(fused_kernel, seq_count // 2, chips, pieces, whole),
        out_shape=[
            vmem((tokens, inner), BF16),
            vmem((tokens, block), BF16),
        ],
        in_specs=[SMEM] + [ANY] * 7,
        out_specs=[pl.BlockSpec(memory_space=vmem)] * 2,
        scratch_shapes=[
            vmem((tokens, inner), BF16), vmem((tokens, inner), BF16),
            vmem((tokens, wide), BF16), vmem((tokens, wide), BF16),
            vmem((heads, tokens), F32),
            vmem((6, SPAN, heads), F32), vmem((2, heads, SPAN), F32),
            row, row,
            square(2), square(2 * groups), square(2 * groups),
            vmem((tokens, inner), BF16), vmem((tokens, inner), BF16),
            vmem((tokens, inner), F32),
            vmem((tokens, wide), F32), vmem((tokens, wide), F32), vmem((tokens, 2 * wide), BF16),
        ]
        + [vmem((inner, STATE), F32)] * 4
        + [vmem((2, inner // 2, STATE), BF16)] * 6
        + [
            vmem((pieces, piece, 2 * wide), BF16),
            vmem(((2 * chips - 1) * summed, piece, 2 * wide), BF16),
            vmem((chips * lead, tokens, piece), BF16),
            vmem((chips * lead, tokens, piece), BF16),
            vmem(((chips - 1) * lead, tokens, piece), BF16),
            vmem(((chips - 1) * lead, tokens, piece), BF16),
            dma((11,)), dma((2,)), dma((3, 2)), dma((3, 2, chunks // 2)),
            dma((2,)), dma((1,)), dma((chips * lead,)), dma((1,)), dma(((chips - 1) * lead,)),
        ]
        + ([
            vmem((whole, piece, 2 * wide), BF16),
            vmem((2, whole, piece, 2 * wide), BF16),
            vmem((3, tokens, 2 * wide), BF16),
            dma((2,)), dma((3,)), dma((5,)), dma((3 + groups,)),
            vmem((piece // 2, 2 * wide), BF16), vmem((2, piece // 2, 2 * wide), BF16),
            vmem((chips, tokens, piece // 2), BF16), vmem((chips, tokens, piece // 2), BF16),
            vmem((tokens, piece // 2), BF16), vmem((tokens, piece // 2), BF16), dma((9,)),
        ] if whole else []),
        compiler_params=pltpu.CompilerParams(
            collective_id=0, has_side_effects=True, vmem_limit_bytes=56 * 1024 * 1024
        ),
        name="fused",
    )(doc_lengths, inner_x, out_grad, in_b, in_c, log_decay, w_b, w_c)
    return tuple(pl.pallas_call(
        store_kernel,
        out_shape=[
            jax.ShapeDtypeStruct((tokens, inner), BF16),
            jax.ShapeDtypeStruct((tokens, block), BF16),
        ],
        in_specs=[pl.BlockSpec(memory_space=vmem)] * 2,
        out_specs=[ANY] * 2,
        scratch_shapes=[dma((2, 1))],
        name="store",
    )(pltpu.with_memory_space_constraint(held_x, pltpu.VMEM), pltpu.with_memory_space_constraint(held_input, pltpu.VMEM)))


def solution(mesh):
    placed = (
        P("seq", "tp"),
        P("seq", "tp"),
        P("seq", "tp"),
        P("tp", "seq"),
        P(),
        P("seq", "tp"),
        P(None, "tp"),
        P(None, "tp"),
    )
    return jax.shard_map(
        per_device,
        mesh=mesh,
        in_specs=placed,
        out_specs=(P("seq", "tp"), P("seq", "tp")),
        check_vma=False,
    )
```

```python
import functools

import jax
import jax.numpy as jnp
from jax import lax
from jax.experimental import pallas as pl
from jax.experimental.pallas import tpu as pltpu
from jax.sharding import PartitionSpec as P

HEAD_DIM = 64
STATE = 128
SPAN = 128
FIRST = 9
SLOT = 2
HOP = 3
WAIT = 8
EDGE_RELAY = 30
LATER = 6
INNER_RELAY = 36
F32 = jnp.float32
BF16 = jnp.bfloat16
MESH = pl.DeviceIdType.MESH
SMEM = pl.BlockSpec(memory_space=pltpu.SMEM)
ANY = pl.BlockSpec(memory_space=pl.ANY)


def dot(a, b, a_dim, b_dim):
    return lax.dot_general(a, b, (((a_dim,), (b_dim,)), ((), ())), preferred_element_type=F32)


def doc_of(lens_ref, position):
    end = 0
    doc = jnp.zeros_like(position)
    for k in range(lens_ref.shape[0] - 1):
        end = end + lens_ref[k]
        doc = doc + (position >= end).astype(jnp.int32)
    return doc


def span_decays(lens_ref, log_ref, number):
    heads, tokens = log_ref.shape
    first = lax.axis_index("seq") * tokens + number * SPAN
    cumulative = log_ref[:, number * SPAN : (number + 1) * SPAN]
    lane = lax.broadcasted_iota(jnp.int32, (heads, SPAN), 1)
    shift = 1
    while shift < SPAN:
        rolled = pltpu.roll(cumulative, shift, 1)
        cumulative = cumulative + jnp.where(lane >= shift, rolled, 0.0)
        shift *= 2
    doc_row = doc_of(lens_ref, first + lane)
    doc_last = doc_of(lens_ref, jnp.full((heads, SPAN), first + SPAN - 1, jnp.int32))
    before = jnp.full((heads, SPAN), first - 1, jnp.int32)
    doc_prior = jnp.where(before >= 0, doc_of(lens_ref, before), -1)
    last = jnp.broadcast_to(cumulative[:, SPAN - 1 :], (heads, SPAN))
    enter = jnp.where(doc_row == doc_prior, jnp.exp(cumulative), 0.0)
    leave = jnp.where(doc_row == doc_last, jnp.exp(last - cumulative), 0.0)
    total = jnp.where(doc_last == doc_prior, jnp.exp(last), 0.0)
    return cumulative, enter, leave, total


def fused_kernel(
    columns, chips, pieces, whole, lens_ref, x_hbm, dy_hbm, b_hbm, c_hbm, log_hbm, wb_ref, wc_ref, gx_ref, out_ref,
    x_ref, dy_ref, b_ref, c_ref, log_ref, turned, totals, d_ref, d_near, bias, scores, mixed,
    xw_ref, dyw_ref, gx_local, gb_ref, gc_ref, gbc_ref, f0_ref, f_ref, g1_ref, g_ref,
    chain_in, chain_out, own_out, near_in, mid_out, start_in,
    w_own, w_far, pair_out, pair_in, chip_out, chip_in,
    load_sems, d_sems, send_sems, recv_sems,
    w_sems, pair_send, pair_recv, chip_send, chip_recv,
    *shared,
):
    summed = pieces - whole
    if whole:
        w_mate, w_cross, gbc_in, mate_sems, cross_sems, relay_sems, gbc_sems = shared[:7]
        mate_part, cross_part, pair_part_out, pair_part_in, chip_part_out, chip_part_in, part_sems = shared[7:]
    lead = summed - 1 if whole else summed
    heads = log_ref.shape[0]
    groups = b_ref.shape[1] // STATE
    chunks = heads // 2
    pairs = chunks // groups
    width = 2 * HEAD_DIM
    k = lax.axis_index("seq")
    m = k // 2
    r = k - 2 * m
    devices = 2 * columns
    partner = k + 1 - 2 * r
    t = lax.axis_index("tp")
    chip = t // 2
    core = t - 2 * chip
    mate = t + 1 - 2 * core
    block = out_ref.shape[1]
    piece = block // pieces
    depth = wb_ref.shape[1]
    z_at = m - 2 * (m // 2)
    z_mate = k + 2 - 4 * z_at
    here = 2 * z_at + r
    over_y = 2 * z_at + 1 - r
    over_z = 2 * (1 - z_at) + r
    across = 2 * (1 - z_at) + 1 - r

    def place(c):
        if not whole:
            return c
        at = 2 * across
        for first, value in (
            (1, 3 - 2 * r), (2, 5), (3, 7), (4, 2 * here), (5, 2 * r + 1), (6, 2 * over_z), (7, 2 * over_y)
        ):
            at = jnp.where(c >= first, value, at)
        return at

    quarter = x_ref.shape[1] // 4
    loads = [
        pltpu.make_async_copy(log_hbm, log_ref, load_sems.at[0]),
        pltpu.make_async_copy(b_hbm, b_ref, load_sems.at[1]),
        pltpu.make_async_copy(c_hbm, c_ref, load_sems.at[2]),
    ]
    for q in range(4):
        cols = pl.ds(q * quarter, quarter)
        loads.append(pltpu.make_async_copy(x_hbm.at[:, cols], x_ref.at[:, cols], load_sems.at[3 + 2 * q]))
        loads.append(pltpu.make_async_copy(dy_hbm.at[:, cols], dy_ref.at[:, cols], load_sems.at[4 + 2 * q]))
    for load in loads:
        load.start()

    barrier = pltpu.get_barrier_semaphore()
    pl.semaphore_signal(barrier, inc=1, device_id={"seq": partner, "tp": t}, device_id_type=MESH)
    for offset in (-2, 2):
        @pl.when(jnp.logical_and(k + offset >= 0, k + offset < devices))
        def _():
            pl.semaphore_signal(
                barrier, inc=1, device_id={"seq": k + offset, "tp": t}, device_id_type=MESH
            )

    def owner_of(offset, same_core):
        at = lax.rem(chip + offset, chips)
        return 2 * at + (core if same_core else 1 - core)

    pl.semaphore_signal(barrier, inc=1, device_id={"seq": k, "tp": mate}, device_id_type=MESH)
    for offset in range(1, chips):
        pl.semaphore_signal(
            barrier, inc=1, device_id={"seq": k, "tp": owner_of(offset, True)}, device_id_type=MESH
        )
    if whole:
        pl.semaphore_signal(
            barrier, inc=1, device_id={"seq": k, "tp": owner_of(1, False)}, device_id_type=MESH
        )


    def rows_of(offset, same_core, c):
        at = owner_of(offset, same_core) * block + place(c) * piece
        return pl.ds(pl.multiple_of(at, piece), piece)

    def halves(which):
        return pl.ds(which * depth, depth)

    def far_slot(offset, same_core, c):
        return (2 * offset - (1 if offset else 0) + (1 if same_core else 0)) * summed + c

    def w_copy(offset, same_core, c, which):
        own = offset == 0 and same_core
        slot = c if own else far_slot(offset, same_core, c)
        return pltpu.make_async_copy(
            (wb_ref, wc_ref)[which].at[rows_of(offset, same_core, c)],
            (w_own if own else w_far).at[slot, :, halves(which)],
            w_sems.at[0 if own else 1],
        )

    def mate_weights(g, which):
        return pltpu.make_async_remote_copy(
            src_ref=(wb_ref, wc_ref)[which].at[rows_of(0, False, summed + g)],
            dst_ref=w_mate.at[g, :, halves(which)],
            send_sem=mate_sems.at[0], recv_sem=mate_sems.at[1],
            device_id={"seq": k, "tp": mate}, device_id_type=MESH,
        )

    def cross_weights(g, source, which):
        target = 2 * (1 - chip) + source * core + (1 - source) * (1 - core)
        at = pl.multiple_of(target * block + place(summed + g) * piece, piece)
        return pltpu.make_async_remote_copy(
            src_ref=(wb_ref, wc_ref)[which].at[pl.ds(at, piece)],
            dst_ref=w_cross.at[source, g, :, halves(which)],
            send_sem=cross_sems.at[0], recv_sem=cross_sems.at[1 + g],
            device_id={"seq": k, "tp": target}, device_id_type=MESH,
        )

    def part_weights(source, which):
        target = mate if source is None else 2 * (1 - chip) + source * core + (1 - source) * (1 - core)
        at = pl.multiple_of(target * block + place(lead) * piece + piece // 2, piece // 2)
        to = mate_part if source is None else cross_part.at[source]
        first = 2 if source is None else 0
        return pltpu.make_async_remote_copy(
            src_ref=(wb_ref, wc_ref)[which].at[pl.ds(at, piece // 2)], dst_ref=to.at[:, halves(which)],
            send_sem=part_sems.at[first], recv_sem=part_sems.at[first + 1],
            device_id={"seq": k, "tp": target}, device_id_type=MESH,
        )

    def relay_weights(source, g):
        return pltpu.make_async_remote_copy(
            src_ref=w_cross.at[source, 1 if g == 1 else 0], dst_ref=w_cross.at[source, g],
            send_sem=relay_sems.at[0], recv_sem=relay_sems.at[1 + source if g == 3 else 2 + g],
            device_id={"seq": partner if g == 3 else z_mate, "tp": t}, device_id_type=MESH,
        )

    def group_columns(group, half):
        return pl.ds(half * groups * STATE + group * STATE, STATE)

    def gbc_copy(kind, group, half):
        cols = group_columns(group, half)
        source = gbc_in.at[1] if kind == 2 else gbc_ref
        return pltpu.make_async_remote_copy(
            src_ref=source.at[:, cols], dst_ref=gbc_in.at[kind, :, cols],
            send_sem=gbc_sems.at[0], recv_sem=gbc_sems.at[3 + group if kind == 1 else 1 + kind // 2],
            device_id={"seq": k, "tp": owner_of(1, True) if kind == 1 else mate}, device_id_type=MESH,
        )

    loads[0].wait()
    low = lax.broadcasted_iota(jnp.int32, (SPAN, width), 1) < HEAD_DIM
    low_mask = low.astype(F32).astype(BF16)
    high_mask = (1.0 - low.astype(F32)).astype(BF16)
    row_id = lax.broadcasted_iota(jnp.int32, (SPAN, SPAN), 0)
    col_id = lax.broadcasted_iota(jnp.int32, (SPAN, SPAN), 1)
    for number in range(2):
        cumulative, enter, leave, total = span_decays(lens_ref, log_ref, number)
        log_ref[:, number * SPAN : (number + 1) * SPAN] = cumulative
        turned[3 * number] = jnp.transpose(cumulative)
        turned[3 * number + 1] = jnp.transpose(enter)
        turned[3 * number + 2] = jnp.transpose(leave)
        totals[number] = total
        first = k * log_ref.shape[1] + number * SPAN
        same = jnp.logical_and(
            doc_of(lens_ref, first + row_id) == doc_of(lens_ref, first + col_id), row_id >= col_id
        )
        bias[number] = jnp.where(same, 0.0, -1e30)
    both = totals[0] * totals[1]
    for h in range(heads):
        d_ref[h] = both[h : h + 1, :]

    count = 1 + jnp.minimum(m, 1) + jnp.minimum(columns - 1 - m, 1) + chips + (1 if whole else 0)
    pl.semaphore_wait(barrier, count)

    def copy(kind, way, j, source, target, to):
        rows = pl.ds(pl.multiple_of(j * width, width), width)
        return pltpu.make_async_remote_copy(
            src_ref=source.at[way, rows], dst_ref=target.at[way, rows],
            send_sem=send_sems.at[kind, way], recv_sem=recv_sems.at[kind, way, j],
            device_id={"seq": to, "tp": t}, device_id_type=MESH,
        )

    def settle(held, sem):
        pltpu.make_async_copy(held, held, sem).wait()

    decays = pltpu.make_async_remote_copy(
        src_ref=d_ref, dst_ref=d_near, send_sem=d_sems.at[0], recv_sem=d_sems.at[1],
        device_id={"seq": partner, "tp": t}, device_id_type=MESH,
    )
    decays.start()

    if whole:
        for which in (0, 1):
            for source in (0, 1):
                cross_weights(0, source, which).start()
        for which in (0, 1):
            cross_weights(1, z_at, which).start()

    loads[1].wait()
    loads[2].wait()

    def fetch_weights():
        for offset in range(chips):
            for same_core in (False, True):
                def fetch(c, carry):
                    for which in (0, 1):
                        w_copy(offset, same_core, c, which).start()
                    return carry

                lax.fori_loop(0, pieces if offset == 0 and same_core else summed, fetch, 0)

    def spans(number):
        return slice(number * SPAN, (number + 1) * SPAN)

    def spread(kind, number, pair):
        held = turned.at[3 * number + kind]
        one = jnp.broadcast_to(held[:, 2 * pair : 2 * pair + 1], (SPAN, width))
        two = jnp.broadcast_to(held[:, 2 * pair + 1 : 2 * pair + 2], (SPAN, width))
        return jnp.where(low, one, two)

    def by_head(number, pair):
        return jnp.concatenate(
            [
                jnp.broadcast_to(totals[number, h : h + 1, :], (HEAD_DIM, STATE))
                for h in (2 * pair, 2 * pair + 1)
            ],
            axis=0,
        )

    def summarize(pair):
        group = pair // pairs
        cols = slice(pair * width, (pair + 1) * width)
        cols_g = slice(group * STATE, (group + 1) * STATE)
        states, grads = [], []
        for number in (0, 1):
            tokens = spans(number)
            x_weighted = (x_ref[tokens, cols].astype(F32) * spread(2, number, pair)).astype(BF16)
            dy_weighted = (dy_ref[tokens, cols].astype(F32) * spread(1, number, pair)).astype(BF16)
            xw_ref[tokens, cols] = x_weighted
            dyw_ref[tokens, cols] = dy_weighted
            states.append(dot(x_weighted, b_ref[tokens, cols_g], 0, 0))
            grads.append(dot(dy_weighted, c_ref[tokens, cols_g], 0, 0))
        f0_ref[cols] = states[0]
        f_ref[cols] = states[1] + by_head(1, pair) * states[0]
        g1_ref[cols] = grads[1]
        g_ref[cols] = grads[0] + by_head(0, pair) * grads[1]

    def local(pair):
        group = pair // pairs
        cols = slice(pair * width, (pair + 1) * width)
        cols_g = slice(group * STATE, (group + 1) * STATE)
        for number in (0, 1):
            tokens = spans(number)
            slot = 2 * group + number
            if pair == group * pairs:
                scores[slot] = dot(c_ref[tokens, cols_g], b_ref[tokens, cols_g], 1, 1)
            x_part, dy_part = x_ref[tokens, cols], dy_ref[tokens, cols]
            x_blocks = jnp.concatenate([x_part * low_mask, x_part * high_mask], axis=0)
            dy_blocks = jnp.concatenate([dy_part * low_mask, dy_part * high_mask], axis=0)
            dots = dot(dy_part, x_blocks, 1, 1)
            score_low = []
            added = None
            for e in range(2):
                h = 2 * pair + e
                column = jnp.broadcast_to(turned[3 * number, :, h : h + 1], (SPAN, SPAN))
                gap = column - log_ref[h : h + 1, number * SPAN : (number + 1) * SPAN]
                within = jnp.exp(gap + bias[number])
                term = within * dots[:, e * SPAN : (e + 1) * SPAN]
                added = term if added is None else added + term
                score_low.append((within * scores[slot]).astype(BF16))
            mixed[slot] = added if pair == group * pairs else mixed[slot] + added
            gx_local[tokens, cols] = dot(jnp.concatenate(score_low, axis=0), dy_blocks, 0, 0)
            if pair == group * pairs + pairs - 1:
                mixed_low = mixed[slot].astype(BF16)
                gb_ref[tokens, cols_g] = dot(mixed_low, c_ref[tokens, cols_g], 0, 0)
                gc_ref[tokens, cols_g] = dot(mixed_low, b_ref[tokens, cols_g], 1, 0)

    def stream(way, source):
        first = r == way
        second = jnp.logical_not(first)
        has_in = (m < columns - 1) if way else (m > 0)
        has_next = (m > 0) if way else (m < columns - 1)
        gives = jnp.logical_or(first, has_next)
        own = lambda j: copy(0, way, j, own_out, near_in, partner)
        chain = lambda j: copy(1, way, j, chain_out, chain_in, k - 2 if way else k + 2)
        middle = lambda j: copy(2, way, j, mid_out, start_in, partner)
        passed = lambda j: copy(2, way, j, chain_in, start_in, partner)

        @pl.when(jnp.logical_not(has_in))
        def _():
            chain_in[way] = jnp.zeros(chain_in.shape[1:], BF16)

        def part(j, e):
            rows = pl.ds(pl.multiple_of(j * width + e * HEAD_DIM, HEAD_DIM), HEAD_DIM)
            held = pl.ds(pl.multiple_of((2 * j + r) * width + e * HEAD_DIM, HEAD_DIM), HEAD_DIM)
            return rows, held, 2 * (2 * j + r) + e

        def give(j):
            @pl.when(gives)
            def _():
                away = pl.ds(pl.multiple_of((2 * j + 1 - r) * width, width), width)
                own_out[way, j * width : (j + 1) * width] = source[away, :].astype(BF16)
                own(j).start()

        def step(j):
            @pl.when(has_in)
            def _():
                chain(j).wait_recv()

            @pl.when(first)
            def _():
                for e in range(2):
                    rows, held, h = part(j, e)
                    mid_out[way, rows] = (
                        source[held, :] + d_ref[h] * chain_in[way, rows].astype(F32)
                    ).astype(BF16)
                middle(j).start()

                @pl.when(has_next)
                def _():
                    own(j).wait_recv()
                    for e in range(2):
                        rows, held, h = part(j, e)
                        mid = source[held, :] + d_ref[h] * chain_in[way, rows].astype(F32)
                        chain_out[way, rows] = (
                            near_in[way, rows].astype(F32) + d_near[h] * mid
                        ).astype(BF16)
                    chain(j).start()

                for e in range(2):
                    rows, held, h = part(j, e)
                    source[held, :] = chain_in[way, rows].astype(F32)

            @pl.when(second)
            def _():
                @pl.when(has_in)
                def _():
                    passed(j).start()

                own(j).wait_recv()

                @pl.when(has_next)
                def _():
                    for e in range(2):
                        rows, held, h = part(j, e)
                        mid = near_in[way, rows].astype(F32) + d_near[h] * chain_in[way, rows].astype(F32)
                        chain_out[way, rows] = (source[held, :] + d_ref[h] * mid).astype(BF16)
                    chain(j).start()

                for e in range(2):
                    rows, held, h = part(j, e)
                    source[held, :] = (
                        near_in[way, rows].astype(F32) + d_near[h] * chain_in[way, rows].astype(F32)
                    )

        def finish(c):
            j = c // 2
            rows = slice(c * width, (c + 1) * width)
            away = r == 1 - c % 2
            arrives = jnp.logical_or(second, has_in)

            @pl.when(jnp.logical_and(away, arrives))
            def _():
                middle(j).wait_recv()
                source[rows, :] = start_in[way, j * width : (j + 1) * width].astype(F32)

            @pl.when(jnp.logical_and(away, jnp.logical_not(arrives)))
            def _():
                source[rows, :] = jnp.zeros((width, STATE), F32)

        def drain():
            @pl.when(gives)
            def _():
                settle(own_out.at[way], send_sems.at[0, way])

            @pl.when(has_next)
            def _():
                settle(chain_out.at[way], send_sems.at[1, way])

            @pl.when(jnp.logical_or(first, has_in))
            def _():
                settle(mid_out.at[way], send_sems.at[2, way])

        return give, step, finish, drain

    forward_give, forward, forward_end, forward_drain = stream(0, f_ref)
    backward_give, backward, backward_end, backward_drain = stream(1, g_ref)

    def carried(pair):
        group = pair // pairs
        cols = slice(pair * width, (pair + 1) * width)
        cols_g = slice(group * STATE, (group + 1) * STATE)
        forward_end(pair)
        backward_end(pair)
        arrived, ended = f_ref[cols], g_ref[cols]
        starts = [arrived.astype(BF16), (f0_ref[cols] + by_head(0, pair) * arrived).astype(BF16)]
        ends = [(g1_ref[cols] + by_head(1, pair) * ended).astype(BF16), ended.astype(BF16)]
        for number in (0, 1):
            tokens = spans(number)
            grad_x = gx_local[tokens, cols] + spread(2, number, pair) * dot(
                b_ref[tokens, cols_g], ends[number], 1, 1
            )
            gx_ref[tokens, cols] = grad_x.astype(BF16)
            gb_ref[tokens, cols_g] += dot(xw_ref[tokens, cols], ends[number], 1, 0)
            gc_ref[tokens, cols_g] += dot(dyw_ref[tokens, cols], starts[number], 1, 0)
        if pair == group * pairs + pairs - 1:
            for half in (0, 1):
                at = (half * groups + group) * STATE
                gbc_ref[:, at : at + STATE] = (gc_ref if half else gb_ref)[:, cols_g].astype(BF16)
                if whole:
                    gbc_copy(1, group, half).start()
                    gbc_copy(0, group, half).start()

    per_load = max(chunks // 4, 1)
    rounds = chunks // 2
    last = HOP * (columns - 1)

    def exchange(e):
        f = e - HOP * m
        b = e - HOP * (columns - 1 - m)

        @pl.when(jnp.logical_and(f >= 0, f < rounds))
        def _():
            forward(f)

        @pl.when(jnp.logical_and(b >= 0, b < rounds))
        def _():
            backward(b)

    early = 2 * m < columns

    def give(j, soon):
        @pl.when(early if soon else jnp.logical_not(early))
        def _():
            forward_give(j)

        @pl.when(jnp.logical_not(early) if soon else early)
        def _():
            backward_give(j)

    edge = jnp.logical_or(m == 0, m == columns - 1)
    done = 0
    for s in range(FIRST + SLOT * (last + rounds) + WAIT):
        if s == min(3, chunks - 1):
            fetch_weights()
            if whole:
                for which in (0, 1):
                    for source in (0, 1, None):
                        part_weights(source, which).start()
                for g in range(whole):
                    for which in (0, 1):
                        mate_weights(g, which).start()
        if s < chunks:
            if s % per_load == 0:
                loads[3 + 2 * (s // per_load)].wait()
                loads[4 + 2 * (s // per_load)].wait()
            summarize(s)
            if s % 2:
                give(s // 2, True)
        behind = s - LATER
        if behind >= 0 and behind % 2 == 1 and behind < chunks:
            give(behind // 2, False)
        e = (s - FIRST) // SLOT
        if s >= FIRST and (s - FIRST) % SLOT == 0 and e < last + rounds:
            if e == 0:
                decays.wait_recv()
            exchange(e)
        if chunks <= s < 2 * chunks:
            local(s - chunks)
        if whole and s == EDGE_RELAY:
            settle(w_cross.at[:, 0], cross_sems.at[1])
        for at, sends in ((EDGE_RELAY, edge), (INNER_RELAY, jnp.logical_not(edge))):
            if whole and s == at:
                @pl.when(sends)
                def _():
                    for source in (0, 1):
                        relay_weights(source, 2).start()
        if whole and s == INNER_RELAY:
            settle(w_cross.at[0, 1], cross_sems.at[2])
            relay_weights(z_at, 1).start()
        ready = s - FIRST - SLOT * last - WAIT
        if s >= 2 * chunks - 1 and ready >= 0:
            while done < chunks and done < 2 * (ready // SLOT + 1):
                carried(done)
                done += 1
    while done < chunks:
        carried(done)
        done += 1


    def relay_group(group):
        settle(gbc_in.at[1, :, pl.ds(0, 2 * STATE)], gbc_sems.at[3 + group])
        for half in (0, 1):
            gbc_copy(2, group, half).start()

    settle(w_own, w_sems.at[0])
    settle(w_far, w_sems.at[1])

    if whole:
        for source in (0, 1):
            relay_weights(source, 3).start()

    def pair_copy(offset, c):
        slot = offset * lead + c
        return pltpu.make_async_remote_copy(
            src_ref=pair_out.at[slot], dst_ref=pair_in.at[slot],
            send_sem=pair_send.at[0], recv_sem=pair_recv.at[slot],
            device_id={"seq": k, "tp": mate}, device_id_type=MESH,
        )

    def chip_copy(offset, c):
        slot = (offset - 1) * lead + c
        return pltpu.make_async_remote_copy(
            src_ref=chip_out.at[slot], dst_ref=chip_in.at[slot],
            send_sem=chip_send.at[0], recv_sem=chip_recv.at[slot],
            device_id={"seq": k, "tp": owner_of(offset, True)}, device_id_type=MESH,
        )

    def partial(offset, same_core, c):
        weights = w_own[c] if offset == 0 and same_core else w_far[far_slot(offset, same_core, c)]
        return dot(gbc_ref[...], weights, 1, 1)

    def give(offset, c):
        pair_out[offset * lead + c] = partial(offset, False, c).astype(BF16)
        pair_copy(offset, c).start()

    def send_on(offset, c):
        own = partial(offset, True, c)
        pair_copy(offset, c).wait_recv()
        slot = offset * lead + c
        chip_out[(offset - 1) * lead + c] = (own + pair_in[slot].astype(F32)).astype(BF16)
        chip_copy(offset, c).start()

    def pair_part(offset):
        return pltpu.make_async_remote_copy(
            src_ref=pair_part_out.at[offset], dst_ref=pair_part_in.at[offset],
            send_sem=part_sems.at[4], recv_sem=part_sems.at[5 + offset],
            device_id={"seq": k, "tp": mate}, device_id_type=MESH,
        )

    def chip_part():
        return pltpu.make_async_remote_copy(
            src_ref=chip_part_out, dst_ref=chip_part_in,
            send_sem=part_sems.at[7], recv_sem=part_sems.at[8],
            device_id={"seq": k, "tp": owner_of(1, True)}, device_id_type=MESH,
        )

    low_rows, high_rows = pl.ds(0, piece // 2), pl.ds(piece // 2, piece // 2)

    def give_part(offset):
        weights = w_far[far_slot(offset, False, lead), low_rows]
        pair_part_out[offset] = dot(gbc_ref[...], weights, 1, 1).astype(BF16)
        pair_part(offset).start()

    if whole:
        give_part(1)

    for offset in range(1, chips):
        def body(s, carry):
            @pl.when(s < lead)
            def _():
                give(offset, s)

            @pl.when(s >= 2)
            def _():
                send_on(offset, s - 2)

            return carry

        lax.fori_loop(0, lead + 2, body, 0)

    if whole:
        own = dot(gbc_ref[...], w_far[far_slot(1, True, lead), low_rows], 1, 1)
        pair_part(1).wait_recv()
        chip_part_out[...] = (own + pair_part_in[1].astype(F32)).astype(BF16)
        chip_part().start()

    def near_give(c, carry):
        give(0, c)
        return carry

    lax.fori_loop(0, lead, near_give, 0)
    if whole:
        give_part(0)

    def gather(g, carry):
        total = dot(gbc_ref[...], w_own[summed + g], 1, 1) + dot(gbc_in[0], w_mate[g], 1, 1)
        for source, held in ((0, gbc_in.at[2]), (1, gbc_in.at[1])):
            if not isinstance(g, jax.Array) and g == 3:
                settle(w_cross.at[source, 3], relay_sems.at[1 + source])
            total = total + dot(held[...], w_cross[source, g], 1, 1)
        cols = pl.ds(pl.multiple_of(place(summed + g) * piece, piece), piece)
        out_ref[:, cols] = total.astype(BF16)
        return carry

    if whole:
        for group in range(groups):
            relay_group(group)
        settle(w_mate, mate_sems.at[1])
        settle(gbc_in.at[0], gbc_sems.at[1])
        settle(gbc_in.at[2], gbc_sems.at[2])
        gather(0, 0)
        settle(mate_part, part_sems.at[3])
        settle(cross_part, part_sems.at[1])
        total = dot(gbc_ref[...], w_own[lead, high_rows], 1, 1) + dot(gbc_in[0], mate_part[...], 1, 1)
        total = total + dot(gbc_in[2], cross_part[0], 1, 1) + dot(gbc_in[1], cross_part[1], 1, 1)
        split = place(lead) * piece
        out_ref[:, pl.ds(pl.multiple_of(split + piece // 2, piece // 2), piece // 2)] = total.astype(BF16)

    def final(c, carry):
        total = partial(0, True, c)
        pair_copy(0, c).wait_recv()
        total = total + pair_in[c].astype(F32)
        for offset in range(1, chips):
            chip_copy(offset, c).wait_recv()
            total = total + chip_in[(offset - 1) * lead + c].astype(F32)
        cols = pl.ds(pl.multiple_of(place(c) * piece, piece), piece)
        out_ref[:, cols] = total.astype(BF16)
        return carry

    lax.fori_loop(0, lead - 1 if whole else lead, final, 0)
    if whole:
        settle(w_cross.at[:, 2], relay_sems.at[4])
        gather(2, 0)
        settle(w_cross.at[0, 1], relay_sems.at[3])
        gather(1, 0)
        final(lead - 1, 0)
        gather(3, 0)
        total = dot(gbc_ref[...], w_own[lead, low_rows], 1, 1)
        pair_part(0).wait_recv()
        total = total + pair_part_in[0].astype(F32)
        chip_part().wait_recv()
        total = total + chip_part_in[...].astype(F32)
        out_ref[:, pl.ds(pl.multiple_of(split, piece // 2), piece // 2)] = total.astype(BF16)

    settle(pair_out, pair_send.at[0])
    settle(chip_out, chip_send.at[0])
    if whole:
        settle(w_cross.at[0, pl.ds(0, 3)], cross_sems.at[0])
        settle(w_mate, mate_sems.at[0])
        settle(cross_part, part_sems.at[0])
        settle(mate_part, part_sems.at[2])
        settle(pair_part_out, part_sems.at[4])
        settle(chip_part_out, part_sems.at[7])
        settle(w_own.at[pl.ds(0, 5)], relay_sems.at[0])
        settle(gbc_in, gbc_sems.at[0])
    forward_drain()
    backward_drain()

    decays.wait_send()


def store_kernel(x_ref, input_ref, x_hbm, input_hbm, sems):
    copies = []
    for i, (held, target) in enumerate(((x_ref, x_hbm), (input_ref, input_hbm))):
        part = held.shape[0]
        for n in range(1):
            rows = pl.ds(n * part, part)
            copies.append(pltpu.make_async_copy(held.at[rows], target.at[rows], sems.at[i, n]))
    for copy in copies:
        copy.start()
    for copy in copies:
        copy.wait()


def per_device(inner_x, in_b, in_c, log_decay, doc_lengths, out_grad, w_b, w_c):
    tokens, inner = inner_x.shape
    heads = log_decay.shape[0]
    seq_count, tp_count = lax.axis_size("seq"), lax.axis_size("tp")
    block = w_b.shape[0] // tp_count
    chips = tp_count // 2
    piece = 256
    pieces = block // piece
    chunks = heads // 2
    wide = in_b.shape[1]
    whole = 4 if chips == 2 and pieces == 8 and seq_count % 4 == 0 else 0
    summed = pieces - whole
    lead = summed - 1 if whole else summed
    groups = wide // STATE
    vmem = pltpu.VMEM
    dma = pltpu.SemaphoreType.DMA
    row = vmem((heads, 1, STATE), F32)
    square = lambda n: vmem((n, SPAN, SPAN), F32)
    held_x, held_input = pl.pallas_call(
        functools.partial(fused_kernel, seq_count // 2, chips, pieces, whole),
        out_shape=[
            vmem((tokens, inner), BF16),
            vmem((tokens, block), BF16),
        ],
        in_specs=[SMEM] + [ANY] * 7,
        out_specs=[pl.BlockSpec(memory_space=vmem)] * 2,
        scratch_shapes=[
            vmem((tokens, inner), BF16), vmem((tokens, inner), BF16),
            vmem((tokens, wide), BF16), vmem((tokens, wide), BF16),
            vmem((heads, tokens), F32),
            vmem((6, SPAN, heads), F32), vmem((2, heads, SPAN), F32),
            row, row,
            square(2), square(2 * groups), square(2 * groups),
            vmem((tokens, inner), BF16), vmem((tokens, inner), BF16),
            vmem((tokens, inner), F32),
            vmem((tokens, wide), F32), vmem((tokens, wide), F32), vmem((tokens, 2 * wide), BF16),
        ]
        + [vmem((inner, STATE), F32)] * 4
        + [vmem((2, inner // 2, STATE), BF16)] * 6
        + [
            vmem((pieces, piece, 2 * wide), BF16),
            vmem(((2 * chips - 1) * summed, piece, 2 * wide), BF16),
            vmem((chips * lead, tokens, piece), BF16),
            vmem((chips * lead, tokens, piece), BF16),
            vmem(((chips - 1) * lead, tokens, piece), BF16),
            vmem(((chips - 1) * lead, tokens, piece), BF16),
            dma((11,)), dma((2,)), dma((3, 2)), dma((3, 2, chunks // 2)),
            dma((2,)), dma((1,)), dma((chips * lead,)), dma((1,)), dma(((chips - 1) * lead,)),
        ]
        + ([
            vmem((whole, piece, 2 * wide), BF16),
            vmem((2, whole, piece, 2 * wide), BF16),
            vmem((3, tokens, 2 * wide), BF16),
            dma((2,)), dma((3,)), dma((5,)), dma((3 + groups,)),
            vmem((piece // 2, 2 * wide), BF16), vmem((2, piece // 2, 2 * wide), BF16),
            vmem((chips, tokens, piece // 2), BF16), vmem((chips, tokens, piece // 2), BF16),
            vmem((tokens, piece // 2), BF16), vmem((tokens, piece // 2), BF16), dma((9,)),
        ] if whole else []),
        compiler_params=pltpu.CompilerParams(
            collective_id=0, has_side_effects=True, vmem_limit_bytes=56 * 1024 * 1024
        ),
        name="fused",
    )(doc_lengths, inner_x, out_grad, in_b, in_c, log_decay, w_b, w_c)
    return tuple(pl.pallas_call(
        store_kernel,
        out_shape=[
            jax.ShapeDtypeStruct((tokens, inner), BF16),
            jax.ShapeDtypeStruct((tokens, block), BF16),
        ],
        in_specs=[pl.BlockSpec(memory_space=vmem)] * 2,
        out_specs=[ANY] * 2,
        scratch_shapes=[dma((2, 1))],
        name="store",
    )(pltpu.with_memory_space_constraint(held_x, pltpu.VMEM), pltpu.with_memory_space_constraint(held_input, pltpu.VMEM)))


def solution(mesh):
    placed = (
        P("seq", "tp"),
        P("seq", "tp"),
        P("seq", "tp"),
        P("tp", "seq"),
        P(),
        P("seq", "tp"),
        P(None, "tp"),
        P(None, "tp"),
    )
    return jax.shard_map(
        per_device,
        mesh=mesh,
        in_specs=placed,
        out_specs=(P("seq", "tp"), P("seq", "tp")),
        check_vma=False,
    )
```
